256 devices in a mesh: img: 32 (over z, y_hi, core), ori: 8 (over x, y_lo).
Axes of the slice: x: 4, y: 4 (y_hi: 2, y_lo: 2; y = y_hi * 2 + y_lo), z: 8, core: 2. Of those that a mesh axis runs over, the one named last changes fastest.
Arguments:
- images: float32 [32768, 2048], P(('img', 'ori')), may hold values from -40 to 40
- precision: float32 [32768], P('img'), may hold values from 0.5 to 2
- projections: bfloat16 [8192, 2048], P('ori'), may hold values from -1 to 1
- tile_mask: int32 [256, 64], P('img', 'ori'), may hold values from 0 to 1, as said below
Outputs:
- posteriors: bfloat16 [32768, 8192], P('img', 'ori')
- references: float32 [8192, 2048], P(('ori', 'img'))
The draws below stay inside these ranges and needn't reach their ends.
Inputs may be any that keep to these rules, and one draw needn't show every extreme that they name: `tile_mask`: every image block has at least one live tile.
All inputs are finite; a program needn't handle non-finite values.
Results may differ from the reference program's by a relative error of at most 0.0095.
Values may be sent and summed in bfloat16 or wider, within the bound.
A program may use at most 64 MiB of HBM per device.

```python
import math
import jax
import jax.numpy as jnp
from jax import lax

K = 2048
ORIENT = 8192
TILE = 128
IMG_DEV = 128
IMAGES = 32768
BLOCKS = 256
TILES = 64
N_IMG = 32
N_ORI = 8


def unit_table(key):
    table = jax.random.normal(jax.random.fold_in(key, 101), (ORIENT, K), jnp.float32)
    return table / jnp.sqrt(jnp.sum(table * table, axis=1, keepdims=True))


def draw_projections(key, part):
    table = unit_table(key)
    return table.astype(jnp.bfloat16)


def draw_images(key, part):
    noise_key = jax.random.fold_in(key, 102)
    result = jax.random.normal(noise_key, (IMAGES, K), jnp.float32)
    return jnp.clip(result, -40.0, 40.0)


def draw_tile_mask(key, part):
    spread = jax.random.randint(jax.random.fold_in(key, 201), (BLOCKS, 1), 100, 1000)
    cutoff = spread * spread // 1000
    levels = jax.random.randint(jax.random.fold_in(key, 202), (BLOCKS, TILES), 0, 1000)
    forced = jax.random.randint(jax.random.fold_in(key, 203), (BLOCKS, 1), 0, TILES)
    columns = jnp.arange(TILES, dtype=jnp.int32)[None, :]
    return jnp.where((levels < cutoff) | (columns == forced), 1, 0).astype(jnp.int32)


def block_levels(stream_key, dims, shards, smallest, largest):
    level = 1.0
    for dim, parts in shards:
        steps = jax.random.uniform(jax.random.fold_in(jax.random.fold_in(stream_key, 6), dim), (parts,), jnp.float32, smallest / len(shards), largest / len(shards))
        level = level * jnp.repeat(jnp.exp(steps), dims[dim] // parts).reshape((-1,) + (1,) * (len(dims) - 1 - dim))
    return level


def setup_inputs(seed: int = 0) -> dict:
    arg_keys = jax.random.split(jax.random.key(seed), 5)
    return {
        "images": draw_images(jax.random.fold_in(arg_keys[4], 71), 0),
        "precision": jnp.clip(jnp.exp(math.log(2.0) - 1.3862944 * jax.random.uniform(arg_keys[1], (IMAGES,), jnp.float32) ** block_levels(arg_keys[1], (IMAGES,), ((0, 32),), -0.2, 0.2)), 0.5, 2.0),
        "projections": draw_projections(jax.random.fold_in(arg_keys[4], 71), 0),
        "tile_mask": draw_tile_mask(jax.random.fold_in(arg_keys[4], 71), 0),
    }


prior_weight = 1.0


def reference(images, precision, projections, tile_mask):
    group_rows = IMG_DEV * N_ORI
    proj_float = projections.astype(jnp.float32)
    squared = jnp.sum(proj_float * proj_float, axis=1)

    def one_group(running, group_index):
        sums_now, counts_now = running
        first_row = (group_index * group_rows).astype(jnp.int32)
        lowered = lax.dynamic_slice_in_dim(images, first_row, group_rows, 0).astype(jnp.bfloat16)
        weights_here = lax.dynamic_slice_in_dim(precision, first_row, group_rows, 0)
        mask_rows = lax.dynamic_slice_in_dim(tile_mask, (group_index * N_ORI).astype(jnp.int32), N_ORI, 0)
        alive = jnp.repeat(jnp.repeat(mask_rows > 0, IMG_DEV, axis=0), TILE, axis=1)
        products = lax.dot_general(lowered, projections, (((1,), (1,)), ((), ())), preferred_element_type=jnp.float32)
        scores = weights_here[:, None] * (products - 0.5 * squared[None, :])
        highest = jnp.max(jnp.where(alive, scores, -jnp.inf), axis=1, keepdims=True)
        lifted = jnp.where(alive, jnp.exp(jnp.where(alive, scores - highest, -jnp.inf)), 0.0)
        posterior = (lifted / jnp.sum(lifted, axis=1, keepdims=True)).astype(jnp.bfloat16)
        sums_now = sums_now + lax.dot_general(posterior, lowered, (((0,), (0,)), ((), ())), preferred_element_type=jnp.float32)
        counts_now = counts_now + jnp.sum(posterior.astype(jnp.float32), axis=0)
        return (sums_now, counts_now), posterior

    start_state = (jnp.zeros((ORIENT, K), jnp.float32), jnp.zeros((ORIENT,), jnp.float32))
    (summed, counts), posts = lax.scan(one_group, start_state, jnp.arange(N_IMG, dtype=jnp.int32))
    posteriors = posts.reshape(IMAGES, ORIENT)
    references = (summed + prior_weight * proj_float) / (counts[:, None] + prior_weight)
    return posteriors, references
```

```python
import jax
import jax.numpy as jnp
from jax import lax
from jax.experimental import pallas as pl
from jax.experimental.pallas import tpu as pltpu
from jax.sharding import PartitionSpec as P

MESH = pl.DeviceIdType.MESH
prior_weight = 1.0
very_low = -1e30

X_CHIPS, Y_LOW = 4, 2
Z_CHIPS, Y_HIGH, CORES = 8, 2, 2
GROUP = X_CHIPS * Y_LOW
ROWS = 128
DEPTH = 2048
PER = 32
QUARTERS = CORES * Y_HIGH
QROWS = Z_CHIPS * PER
LANES = 128
PIECES = 4
PIECE = ROWS // PIECES
CHUNKS = ((0, 512, True, "z"), (512, 512, False, "z"), (1024, 512, False, "z"), (1536, 512, False, "z"))
STAT_SLOT = {1: 1, 2: 3, 3: 2, 4: 4, 5: 5, 6: 7, 7: 6}

f32 = jnp.float32
bf16 = jnp.bfloat16


def width_of(chunk):
    return chunk[1] + (LANES if chunk[2] else 0)


def kernel(images, precision, projections, tile_mask, posteriors, references, raw, xbuf, table, half_squares, bias, lifted,
           weights, turned, stat_out, stat_in, load_sem, piece_send, piece_recv, stat_send, stat_recv, post_sem,
           core_send, core_recv, ring_send, ring_recv, y_send, y_recv, *chunk_refs):
    img, ori = lax.axis_index("img"), lax.axis_index("ori")
    z, y_hi, core = img // 4, (img // 2) % 2, img % 2
    x, y_lo = ori // 2, ori % 2

    def at_ori(dx, flip):
        row = 1 - y_lo if flip else y_lo
        return ((x + dx) % X_CHIPS) * 2 + row

    where_from = [at_ori(0, False), at_ori(0, True), at_ori(3, False), at_ori(1, False),
                  at_ori(2, False), at_ori(2, True), at_ori(3, True), at_ori(1, True)]
    peers = [(img, w) for w in where_from]
    y_peer, left, right = peers[1], peers[2], peers[3]
    other_core = (z * 4 + y_hi * 2 + 1 - core, ori)
    z_up = (((z + 1) % Z_CHIPS) * 4 + y_hi * 2 + core, ori)
    z_down = (((z + 7) % Z_CHIPS) * 4 + y_hi * 2 + core, ori)
    y_far = (z * 4 + (1 - y_hi) * 2 + core, ori)

    load_images = pltpu.make_async_copy(images, raw, load_sem.at[4])
    load_images.start()
    load_table = []
    for c in range(CORES):
        for yy in range(Y_HIGH):
            q = c * Y_HIGH + yy
            load_table.append(pltpu.make_async_copy(projections.at[:, yy, c], table.at[q], load_sem.at[q]))
            load_table[-1].start()

    barrier = pltpu.get_barrier_semaphore()
    friends = peers[1:] + [other_core, z_up, z_down, y_far]
    for friend in friends:
        pl.semaphore_signal(barrier, inc=1, device_id=friend, device_id_type=MESH)

    load_images.wait()
    xbuf[0] = raw[...].astype(bf16)
    pl.semaphore_wait(barrier, len(friends))

    sends = []
    arrivals = {}
    counter = [0]

    def send_piece(slot, piece, target, far_slot):
        rows = pl.ds(piece * PIECE, PIECE)
        copy = pltpu.make_async_remote_copy(
            src_ref=xbuf.at[slot, rows], dst_ref=xbuf.at[far_slot, rows], send_sem=piece_send.at[counter[0]],
            recv_sem=piece_recv.at[far_slot, piece], device_id=target, device_id_type=MESH)
        counter[0] += 1
        copy.start()
        sends.append(copy)
        arrivals[(far_slot, piece)] = copy

    def arrived(slot, piece):
        arrivals[(slot, piece)].wait_recv()

    half = PIECES // 2
    for i in range(PIECES):
        send_piece(0, i, y_peer, 1)
        send_piece(0, i, right, 2)
        send_piece(0, (i + half) % PIECES, left, 3)

    for copy in load_table:
        copy.wait()

    def square_tile(q, carry):
        wide = table[q].reshape(QROWS, DEPTH).astype(f32)
        total = jnp.sum(wide * wide, axis=1, keepdims=True)
        half_squares[q] = jnp.broadcast_to(0.5 * total, (QROWS, LANES))
        return carry

    lax.fori_loop(0, QUARTERS, square_tile, 0)

    row_ids = lax.broadcasted_iota(jnp.int32, (GROUP, LANES), 0)
    state = {"high": jnp.zeros((GROUP, LANES), f32), "total": jnp.zeros((GROUP, LANES), f32)}

    def score_pair(p):
        slots = (2 * p, 2 * p + 1)
        wide = 2 * LANES
        cols = pl.ds(p * wide, wide)
        for k, slot in enumerate(slots):
            for zz in range(Z_CHIPS):
                live = jnp.where(tile_mask[where_from[slot], zz] > 0, 0.0, very_low)
                bias[pl.ds(zz * PER, PER), pl.ds(k * LANES, LANES)] = jnp.full((PER, LANES), live, f32)
        scale = jnp.concatenate([precision[pl.ds(where_from[slot], 1), :] for slot in slots], axis=1)

        def score_tile(q, high):
            block = table[q].reshape(QROWS, DEPTH)
            rows = xbuf[pl.ds(2 * p, 2)].reshape(wide, DEPTH)
            products = lax.dot_general(block, rows, (((1,), (1,)), ((), ())), preferred_element_type=f32)
            norm = half_squares[q]
            scores = scale * (products - jnp.concatenate([norm, norm], axis=1)) + bias[...]
            lifted[q, :, cols] = scores
            return jnp.maximum(high, jnp.max(scores.reshape(QROWS // 8, 8, wide), axis=0))

        high = lax.fori_loop(0, QUARTERS, score_tile, jnp.full((8, wide), -3e38, f32))
        high = jnp.max(high, axis=0, keepdims=True)

        def lift_tile(q, total):
            values = jnp.exp(lifted[q, :, cols] - high)
            lifted[q, :, cols] = values
            return total + jnp.sum(values.reshape(QROWS // 8, 8, wide), axis=0)

        total = lax.fori_loop(0, QUARTERS, lift_tile, jnp.zeros((8, wide), f32))
        total = jnp.sum(total, axis=0, keepdims=True)
        for k, slot in enumerate(slots):
            here = row_ids == where_from[slot]
            span = slice(k * LANES, (k + 1) * LANES)
            state["high"] = jnp.where(here, high[:, span], state["high"])
            state["total"] = jnp.where(here, total[:, span], state["total"])

    for i in range(half):
        arrived(2, i)
        send_piece(2, i, right, 4)
        arrived(3, half + i)
        send_piece(3, half + i, left, 4)
    for i in range(PIECES):
        arrived(1, i)
        send_piece(1, i, right, 6)
        send_piece(1, i, left, 7)
    score_pair(0)
    for i in range(half):
        arrived(2, half + i)
        arrived(3, i)
    for i in range(half):
        arrived(4, i)
        send_piece(4, i, y_peer, 5)
        arrived(4, half + i)
        send_piece(4, half + i, y_peer, 5)
    score_pair(1)
    for i in range(PIECES):
        arrived(5, i)
    score_pair(2)
    for i in range(PIECES):
        arrived(6, i)
        arrived(7, i)
    score_pair(3)

    my_high, my_total = state["high"], state["total"]
    stat_out[0:GROUP, :] = my_high
    stat_out[GROUP:2 * GROUP, :] = my_total
    stat_copies = []
    for r in range(1, GROUP):
        copy = pltpu.make_async_remote_copy(
            src_ref=stat_out, dst_ref=stat_in.at[STAT_SLOT[r]], send_sem=stat_send.at[r],
            recv_sem=stat_recv.at[STAT_SLOT[r]], device_id=peers[r], device_id_type=MESH)
        copy.start()
        sends.append(copy)
        stat_copies.append(copy)
    for copy in stat_copies:
        copy.wait_recv()
    highest = my_high
    for r in range(1, GROUP):
        highest = jnp.maximum(highest, stat_in[r, 0:GROUP, :])
    my_part = jnp.exp(my_high - highest)
    whole = my_total * my_part
    for r in range(1, GROUP):
        whole = whole + stat_in[r, GROUP:2 * GROUP, :] * jnp.exp(stat_in[r, 0:GROUP, :] - highest)
    factor = my_part / whole
    factor_rows = [jnp.sum(jnp.where(row_ids == w, factor, 0.0), axis=0, keepdims=True) for w in where_from]
    factor_row = jnp.concatenate(factor_rows, axis=1)

    def weight_tile(q, carry):
        weights[q] = (lifted[q] * factor_row).astype(bf16)
        return carry

    lax.fori_loop(0, QUARTERS, weight_tile, 0)

    post_copies = []

    def give_posteriors(slot):
        span = pl.ds(slot * LANES, LANES)

        def tile(zz, carry):
            rows = pl.ds(pl.multiple_of(zz * PER, PER), PER)
            block = jnp.concatenate([lifted[q, rows, span] for q in (0, 2, 1, 3)], axis=0)
            block = (block * factor_rows[slot]).T
            turned[slot, :, pl.ds(pl.multiple_of(zz * LANES, LANES), LANES)] = block.astype(bf16)
            return carry

        lax.fori_loop(0, Z_CHIPS, tile, 0)
        first = pl.multiple_of(where_from[slot] * ROWS, ROWS)
        copy = pltpu.make_async_copy(turned.at[slot], posteriors.at[pl.ds(first, ROWS), :], post_sem.at[slot])
        copy.start()
        post_copies.append(copy)

    per_chunk = [chunk_refs[i * 7:(i + 1) * 7] for i in range(len(CHUNKS))]
    ring_copies = {}
    core_copies, y_copies = {}, {}
    mine_y = core * Y_HIGH

    def product(chunk, q):
        start, wide, counted, _ = chunk
        block = weights[q]
        rows = xbuf[:, :, pl.ds(start, wide)].reshape(GROUP * ROWS, wide)
        value = jnp.dot(block, rows, preferred_element_type=f32)
        if counted:
            ones = jnp.ones((GROUP * ROWS, LANES), bf16)
            value = jnp.concatenate([value, jnp.dot(block, ones, preferred_element_type=f32)], axis=1)
        return value

    def stage_core(j):
        to_core = per_chunk[j][0]

        def one(yy, carry):
            to_core[yy] = product(CHUNKS[j], (1 - core) * Y_HIGH + yy).astype(bf16)
            return carry

        lax.fori_loop(0, Y_HIGH, one, 0)
        copy = pltpu.make_async_remote_copy(
            src_ref=to_core, dst_ref=per_chunk[j][1], send_sem=core_send.at[j], recv_sem=core_recv.at[j],
            device_id=other_core, device_id_type=MESH)
        copy.start()
        sends.append(copy)
        core_copies[j] = copy

    def ring_start(j, step, up, src, dst):
        d = 0 if up else 1
        copy = pltpu.make_async_remote_copy(
            src_ref=src, dst_ref=dst, send_sem=ring_send.at[j, step, d], recv_sem=ring_recv.at[j, step, d],
            device_id=z_up if up else z_down, device_id_type=MESH)
        copy.start()
        sends.append(copy)
        ring_copies[(j, step, d)] = copy

    def ring_first(j):
        local, out, into = per_chunk[j][2], per_chunk[j][3], per_chunk[j][4]
        rows = local.shape[1]
        mid = rows // 2
        far = (z + 4) % Z_CHIPS
        values = local[far].astype(bf16)
        out[0, 0, 0:mid] = values[0:mid]
        out[0, 1, 0:mid] = values[mid:rows]
        for d in range(2):
            ring_start(j, 0, d == 0, out.at[0, d, pl.ds(0, mid)], into.at[0, d, pl.ds(0, mid)])

    def ring_next(j, step):
        local, out, into = per_chunk[j][2], per_chunk[j][3], per_chunk[j][4]
        rows = local.shape[1]
        mid = rows // 2
        for d in range(2):
            ring_copies[(j, step - 1, d)].wait_recv()
            whose = (z + 4 - step) % Z_CHIPS if d == 0 else (z + 4 + step) % Z_CHIPS
            if step == 1:
                got = into[0, d, 0:mid].astype(f32)
                if d == 0:
                    out[1, d, 0:mid] = (local[whose, 0:mid] + got).astype(bf16)
                    out[1, d, mid:rows] = local[whose, mid:rows].astype(bf16)
                else:
                    out[1, d, 0:mid] = local[whose, 0:mid].astype(bf16)
                    out[1, d, mid:rows] = (local[whose, mid:rows] + got).astype(bf16)
            else:
                out[step, d] = (local[whose] + into[step - 1, d].astype(f32)).astype(bf16)
            ring_start(j, step, d == 0, out.at[step, d], into.at[step, d])

    def ring_sum(j):
        local, into = per_chunk[j][2], per_chunk[j][4]
        for d in range(2):
            ring_copies[(j, 3, d)].wait_recv()
        return local[z] + into[3, 0].astype(f32) + into[3, 1].astype(f32)

    def y_start(j):
        copy = pltpu.make_async_remote_copy(
            src_ref=per_chunk[j][5], dst_ref=per_chunk[j][6], send_sem=y_send.at[j], recv_sem=y_recv.at[j],
            device_id=y_far, device_id_type=MESH)
        copy.start()
        sends.append(copy)
        y_copies[j] = copy

    def stage_local(j):
        from_core, local = per_chunk[j][1], per_chunk[j][2]
        wide = width_of(CHUNKS[j])
        z_first = CHUNKS[j][3] == "z"

        def own(yy):
            value = product(CHUNKS[j], mine_y + yy)
            return (value + from_core[yy].astype(f32)).reshape(Z_CHIPS, PER, wide)

        core_copies[j].wait_recv()
        if z_first:
            for yy in range(Y_HIGH):
                local[:, pl.ds(yy * PER, PER), :] = own(yy)
            ring_first(j)
        else:
            per_chunk[j][5][...] = own(1 - y_hi).astype(bf16)
            y_start(j)
            local[...] = own(y_hi)

    state["divide"] = None

    def finish(j, value):
        start, wide, counted, _ = CHUNKS[j]
        if counted:
            state["divide"] = value[:, wide:wide + LANES] + prior_weight
        below = jnp.concatenate([state["divide"]] * (wide // LANES), axis=1)
        prior = table[mine_y + y_hi, z, :, pl.ds(start, wide)].astype(f32)
        references[:, pl.ds(start, wide)] = (value[:, 0:wide] + prior_weight * prior) / below

    def stages(j):
        if CHUNKS[j][3] == "z":
            def to_y():
                local = per_chunk[j][2]
                local[z] = ring_sum(j)
                per_chunk[j][5][...] = local[z, pl.ds(pl.multiple_of((1 - y_hi) * PER, PER), PER), :].astype(bf16)
                y_start(j)

            def last():
                y_copies[j].wait_recv()
                mine = per_chunk[j][2][z, pl.ds(pl.multiple_of(y_hi * PER, PER), PER), :]
                finish(j, mine + per_chunk[j][6][...].astype(f32))

            return [lambda: stage_core(j), lambda: stage_local(j), lambda: ring_next(j, 1), lambda: ring_next(j, 2),
                    lambda: ring_next(j, 3), to_y, last]

        def add_y():
            y_copies[j].wait_recv()
            local = per_chunk[j][2]
            local[...] = local[...] + per_chunk[j][6][...].astype(f32)
            ring_first(j)

        return [lambda: stage_core(j), lambda: stage_local(j), add_y, lambda: ring_next(j, 1), lambda: ring_next(j, 2),
                lambda: ring_next(j, 3), lambda: finish(j, ring_sum(j))]

    plans = [stages(j) for j in range(len(CHUNKS))]
    depth = len(plans[0])
    for t in range(len(CHUNKS) + depth - 1):
        for j in range(len(CHUNKS)):
            s = t - j
            if 0 <= s < depth:
                plans[j][s]()
        if 3 <= t < 7:
            give_posteriors(2 * (t - 3))
            give_posteriors(2 * (t - 3) + 1)

    for copy in sends:
        copy.wait_send()
    for copy in post_copies:
        copy.wait()


def scratch():
    shapes = [
        pltpu.VMEM((ROWS, DEPTH), f32),
        pltpu.VMEM((GROUP, ROWS, DEPTH), bf16),
        pltpu.VMEM((QUARTERS, Z_CHIPS, PER, DEPTH), bf16),
        pltpu.VMEM((QUARTERS, QROWS, LANES), f32),
        pltpu.VMEM((QROWS, 2 * LANES), f32),
        pltpu.VMEM((QUARTERS, QROWS, GROUP * ROWS), f32),
        pltpu.VMEM((QUARTERS, QROWS, GROUP * ROWS), bf16),
        pltpu.VMEM((GROUP, ROWS, QUARTERS * QROWS), bf16),
        pltpu.VMEM((2 * GROUP, LANES), f32),
        pltpu.VMEM((GROUP, 2 * GROUP, LANES), f32),
        pltpu.SemaphoreType.DMA((5,)),
        pltpu.SemaphoreType.DMA((7 * PIECES,)),
        pltpu.SemaphoreType.DMA((GROUP, PIECES)),
        pltpu.SemaphoreType.DMA((GROUP,)),
        pltpu.SemaphoreType.DMA((GROUP,)),
        pltpu.SemaphoreType.DMA((GROUP,)),
        pltpu.SemaphoreType.DMA((len(CHUNKS),)),
        pltpu.SemaphoreType.DMA((len(CHUNKS),)),
        pltpu.SemaphoreType.DMA((len(CHUNKS), 4, 2)),
        pltpu.SemaphoreType.DMA((len(CHUNKS), 4, 2)),
        pltpu.SemaphoreType.DMA((len(CHUNKS),)),
        pltpu.SemaphoreType.DMA((len(CHUNKS),)),
    ]
    for chunk in CHUNKS:
        wide = width_of(chunk)
        z_first = chunk[3] == "z"
        rows = Y_HIGH * PER if z_first else PER
        y_shape = (PER, wide) if z_first else (Z_CHIPS, PER, wide)
        shapes += [
            pltpu.VMEM((Y_HIGH, QROWS, wide), bf16),
            pltpu.VMEM((Y_HIGH, QROWS, wide), bf16),
            pltpu.VMEM((Z_CHIPS, rows, wide), f32),
            pltpu.VMEM((4, 2, rows, wide), bf16),
            pltpu.VMEM((4, 2, rows, wide), bf16),
            pltpu.VMEM(y_shape, bf16),
            pltpu.VMEM(y_shape, bf16),
        ]
    return shapes


def body(images, precision, projections, tile_mask):
    return pl.pallas_call(
        kernel,
        out_shape=(
            jax.ShapeDtypeStruct((GROUP * ROWS, QUARTERS * QROWS), bf16),
            jax.ShapeDtypeStruct((PER, DEPTH), f32),
        ),
        in_specs=[
            pl.BlockSpec(memory_space=pl.ANY),
            pl.BlockSpec(memory_space=pltpu.VMEM),
            pl.BlockSpec(memory_space=pl.ANY),
            pl.BlockSpec(memory_space=pltpu.SMEM),
        ],
        out_specs=(pl.BlockSpec(memory_space=pl.ANY), pl.BlockSpec(memory_space=pltpu.VMEM)),
        scratch_shapes=scratch(),
        compiler_params=pltpu.CompilerParams(
            collective_id=0, has_side_effects=True, vmem_limit_bytes=60 * 1024 * 1024
        ),
    )(images, precision.reshape(GROUP, ROWS), projections.reshape(Z_CHIPS, Y_HIGH, CORES, PER, DEPTH), tile_mask)


def solution(mesh):
    return jax.shard_map(
        body,
        mesh=mesh,
        in_specs=(P(("img", "ori"), None), P("img"), P("ori", None), P("img", "ori")),
        out_specs=(P("img", "ori"), P(("ori", "img"), None)),
        check_vma=False,
    )
```

```python
import jax
import jax.numpy as jnp
from jax import lax
from jax.experimental import pallas as pl
from jax.experimental.pallas import tpu as pltpu
from jax.sharding import PartitionSpec as P

MESH = pl.DeviceIdType.MESH
prior_weight = 1.0
very_low = -1e30

X_CHIPS, Y_LOW = 4, 2
Z_CHIPS, Y_HIGH, CORES = 8, 2, 2
GROUP = X_CHIPS * Y_LOW
HANDS = 8
ROWS = 128
DEPTH = 2048
PER = 32
QUARTERS = CORES * Y_HIGH
QROWS = Z_CHIPS * PER
LANES = 128
PIECES = 8
STACK = 2
PIECE = DEPTH // PIECES
PIECE_ORDER = (0, 4, 1, 5, 2, 6, 3, 7)
CHUNKS = ((0, 256, False, "z"), (256, 256, False, "y"), (512, 256, False, "z"), (768, 256, False, "z"),
          (1024, 256, True, "y"), (1280, 256, False, "y"), (1536, 256, False, "z"), (1792, 256, False, "z"))
ORDER = (
    (0, 0), (1, 0), (2, 0), (3, 0), (4, 0), (0, 1), (1, 1), (2, 1), (5, 0), (3, 1), (6, 0), (0, 2), (4, 1), (2, 2),
    (5, 1), (6, 1), (3, 2), (7, 0), (0, 3), (1, 2), (2, 3), (7, 1), (6, 2), (3, 3), (0, 4), (1, 3), (2, 4), (7, 2),
    (4, 2), (6, 3), (3, 4), (0, 5), (1, 4), (2, 5), (5, 2), (7, 3), (4, 3), (6, 4), (0, 6), (3, 5), (1, 5), (5, 3),
    (2, 6), (7, 4), (4, 4), (6, 5), (1, 6), (5, 4), (3, 6), (7, 5), (4, 5), (5, 5), (6, 6), (4, 6), (7, 6), (5, 6),
)
STAT_SLOT = {1: 1, 2: 3, 3: 2, 4: 4, 5: 5, 6: 7, 7: 6}

f32 = jnp.float32
bf16 = jnp.bfloat16


def width_of(chunk):
    return chunk[1] + (LANES if chunk[2] else 0)


def kernel(images, precision_hbm, projections, mask_hbm, posteriors, references, precision, tile_mask, raw, xbuf, table, half_squares, bias, lifted,
           weights, turned, given, stat_out, stat_in, load_sem, piece_send, piece_recv, stat_send, stat_recv, post_sem,
           core_send, core_recv, ring_send, ring_recv, y_send, y_recv, *chunk_refs):
    img, ori = lax.axis_index("img"), lax.axis_index("ori")
    z, y_hi, core = img // 4, (img // 2) % 2, img % 2
    x, y_lo = ori // 2, ori % 2

    def at_ori(dx, flip):
        row = 1 - y_lo if flip else y_lo
        return ((x + dx) % X_CHIPS) * 2 + row

    where_from = [at_ori(0, False), at_ori(0, True), at_ori(3, False), at_ori(1, False),
                  at_ori(2, False), at_ori(2, True), at_ori(3, True), at_ori(1, True)]
    peers = [(img, w) for w in where_from]
    y_peer, left, right = peers[1], peers[2], peers[3]
    other_core = (z * 4 + y_hi * 2 + 1 - core, ori)
    z_up = (((z + 1) % Z_CHIPS) * 4 + y_hi * 2 + core, ori)
    z_down = (((z + 7) % Z_CHIPS) * 4 + y_hi * 2 + core, ori)
    y_far = (z * 4 + (1 - y_hi) * 2 + core, ori)

    load_images = []
    for i in PIECE_ORDER:
        span = pl.ds(i * PIECE, PIECE)
        load_images.append(pltpu.make_async_copy(images.at[:, span], raw.at[:, span], load_sem.at[i]))
        load_images[-1].start()
    load_small = [pltpu.make_async_copy(precision_hbm, precision, load_sem.at[PIECES]),
                  pltpu.make_async_copy(mask_hbm, tile_mask, load_sem.at[PIECES + 1])]
    load_table = []
    for c in range(CORES):
        for yy in range(Y_HIGH):
            q = c * Y_HIGH + yy
            load_table.append(
                pltpu.make_async_copy(projections.at[:, yy, c], table.at[q], load_sem.at[PIECES + 2 + q]))

    barrier = pltpu.get_barrier_semaphore()
    friends = peers[1:] + [other_core, z_up, z_down, y_far]
    for friend in friends:
        pl.semaphore_signal(barrier, inc=1, device_id=friend, device_id_type=MESH)

    def lower(place):
        load_images[place].wait()
        span = pl.ds(PIECE_ORDER[place] * PIECE, PIECE)
        xbuf[0, :, span] = raw[:, span].astype(bf16)

    for place in range(2):
        lower(place)
    pl.semaphore_wait(barrier, len(friends))

    sends = []
    arrivals = {}
    counter = [0]

    def send_piece(slot, piece, target, far_slot):
        span = pl.ds(piece * PIECE, PIECE)
        copy = pltpu.make_async_remote_copy(
            src_ref=xbuf.at[slot, :, span], dst_ref=xbuf.at[far_slot, :, span], send_sem=piece_send.at[counter[0]],
            recv_sem=piece_recv.at[far_slot, piece], device_id=target, device_id_type=MESH)
        counter[0] += 1
        copy.start()
        sends.append(copy)
        arrivals[(far_slot, piece)] = copy

    def arrived(slot, piece):
        arrivals[(slot, piece)].wait_recv()

    half = PIECES // 2
    for i in range(half):
        if i > 0:
            lower(2 * i)
            lower(2 * i + 1)
        send_piece(0, i, right, 2)
        send_piece(0, half + i, left, 3)
        send_piece(0, i, y_peer, 1)
        send_piece(0, half + i, y_peer, 1)
    for i in range(half):
        send_piece(0, half + i, right, 2)
        send_piece(0, i, left, 3)

    for copy in load_small + load_table:
        copy.start()
    for copy in load_small + load_table:
        copy.wait()

    def square_tile(q, carry):
        wide = table[q].reshape(QROWS, DEPTH).astype(f32)
        total = jnp.sum(wide * wide, axis=1, keepdims=True)
        half_squares[q] = jnp.broadcast_to(0.5 * total, (QROWS, LANES))
        return carry

    lax.fori_loop(0, QUARTERS, square_tile, 0)

    row_ids = lax.broadcasted_iota(jnp.int32, (GROUP, LANES), 0)
    state = {"high": jnp.zeros((GROUP, LANES), f32), "total": jnp.zeros((GROUP, LANES), f32)}

    def product_tile(q, slots, spans):
        total = None
        for first, last in spans:
            span = pl.ds(first * PIECE, (last - first) * PIECE)
            block = table[q, :, :, span].reshape(QROWS, (last - first) * PIECE)
            rows = xbuf[pl.ds(slots[0], len(slots)), :, span].reshape(len(slots) * ROWS, (last - first) * PIECE)
            part = lax.dot_general(block, rows, (((1,), (1,)), ((), ())), preferred_element_type=f32)
            total = part if total is None else total + part
        return total

    def partial_score(slots, spans):
        cols = pl.ds(slots[0] * LANES, len(slots) * LANES)

        def tile(t, carry):
            for i in range(STACK):
                q = t * STACK + i
                lifted[q, :, cols] = product_tile(q, slots, spans)
            return carry

        lax.fori_loop(0, QUARTERS // STACK, tile, 0)

    def score(slots, spans=((0, PIECES),), started=False):
        wide = len(slots) * LANES
        cols = pl.ds(slots[0] * LANES, wide)
        for k, slot in enumerate(slots):
            for zz in range(Z_CHIPS):
                live = jnp.where(tile_mask[where_from[slot], zz] > 0, 0.0, very_low)
                bias[pl.ds(zz * PER, PER), pl.ds(k * LANES, LANES)] = jnp.full((PER, LANES), live, f32)
        scale = jnp.concatenate([precision[pl.ds(where_from[slot], 1), :] for slot in slots], axis=1)

        def score_tile(t, high):
            for i in range(STACK):
                q = t * STACK + i
                products = product_tile(q, slots, spans)
                if started:
                    products = products + lifted[q, :, cols]
                norm = jnp.concatenate([half_squares[q]] * len(slots), axis=1)
                scores = scale * (products - norm) + bias[:, 0:wide]
                lifted[q, :, cols] = scores
                high = jnp.maximum(high, jnp.max(scores.reshape(QROWS // 8, 8, wide), axis=0))
            return high

        high = lax.fori_loop(0, QUARTERS // STACK, score_tile, jnp.full((8, wide), -3e38, f32))
        high = jnp.max(high, axis=0, keepdims=True)

        def lift_tile(q, total):
            values = jnp.exp(lifted[q, :, cols] - high)
            lifted[q, :, cols] = values
            return total + jnp.sum(values.reshape(QROWS // 8, 8, wide), axis=0)

        total = lax.fori_loop(0, QUARTERS, lift_tile, jnp.zeros((8, wide), f32))
        total = jnp.sum(total, axis=0, keepdims=True)
        for k, slot in enumerate(slots):
            here = row_ids == where_from[slot]
            span = slice(k * LANES, (k + 1) * LANES)
            state["high"] = jnp.where(here, high[:, span], state["high"])
            state["total"] = jnp.where(here, total[:, span], state["total"])

    def turn(slot):
        span = pl.ds(slot * LANES, LANES)

        def tile(zz, carry):
            rows = pl.ds(pl.multiple_of(zz * PER, PER), PER)
            block = jnp.concatenate([lifted[q, rows, span] for q in (0, 2, 1, 3)], axis=0)
            turned[slot, :, pl.ds(pl.multiple_of(zz * LANES, LANES), LANES)] = block.T
            return carry

        lax.fori_loop(0, Z_CHIPS, tile, 0)

    for i in range(half):
        arrived(2, i)
        send_piece(2, i, right, 4)
        arrived(3, half + i)
        send_piece(3, half + i, left, 4)
        if i == 1:
            score((0,))
    for i in range(half):
        arrived(1, i)
        send_piece(1, i, right, 6)
        arrived(1, half + i)
        send_piece(1, half + i, left, 7)
        arrived(2, half + i)
        send_piece(2, half + i, y_peer, 6)
        arrived(3, i)
        send_piece(3, i, y_peer, 7)
        if i == 0:
            turn(0)
    score((1, 2))
    turn(1)
    turn(2)
    for i in range(half):
        arrived(4, i)
        arrived(4, half + i)
    for i in (half - 1, PIECES - 1):
        send_piece(4, i, y_peer, 5)
    for i in range(2):
        arrived(6, half + i)
        send_piece(6, half + i, right, 5)
        arrived(7, i)
        send_piece(7, i, left, 5)
    score((3, 4))
    arrived(6, half + 2)
    send_piece(6, half + 2, right, 5)
    arrived(7, 2)
    send_piece(7, 2, left, 5)
    turn(3)
    turn(4)
    arrived(6, PIECES - 1)
    arrived(7, half - 1)
    for i in range(half):
        arrived(6, i)
        arrived(7, half + i)
    score((6, 7))
    for i in (4, 0, 5, 1, 3):
        arrived(5, i)
    partial_score((5,), ((0, 2), (3, 6)))
    turn(6)
    for i in (6, 2, 7):
        arrived(5, i)
    score((5,), ((2, 3), (6, 8)), True)

    my_high, my_total = state["high"], state["total"]
    stat_out[0:GROUP, :] = my_high
    stat_out[GROUP:2 * GROUP, :] = my_total
    stat_copies = []
    for r in range(1, GROUP):
        copy = pltpu.make_async_remote_copy(
            src_ref=stat_out, dst_ref=stat_in.at[STAT_SLOT[r]], send_sem=stat_send.at[r],
            recv_sem=stat_recv.at[STAT_SLOT[r]], device_id=peers[r], device_id_type=MESH)
        copy.start()
        sends.append(copy)
        stat_copies.append(copy)
    for slot in (7, 5):
        turn(slot)
    for copy in stat_copies:
        copy.wait_recv()
    highest = my_high
    for r in range(1, GROUP):
        highest = jnp.maximum(highest, stat_in[r, 0:GROUP, :])
    my_part = jnp.exp(my_high - highest)
    whole = my_total * my_part
    for r in range(1, GROUP):
        whole = whole + stat_in[r, GROUP:2 * GROUP, :] * jnp.exp(stat_in[r, 0:GROUP, :] - highest)
    factor = my_part / whole
    factor_rows = [jnp.sum(jnp.where(row_ids == w, factor, 0.0), axis=0, keepdims=True) for w in where_from]
    factor_row = jnp.concatenate(factor_rows, axis=1)

    def weight_tile(q, carry):
        weights[q] = (lifted[q] * factor_row).astype(bf16)
        return carry

    lax.fori_loop(0, QUARTERS, weight_tile, 0)

    post_copies = []

    def give_posteriors(slot):
        columns = jnp.broadcast_to(factor_rows[slot], (LANES, LANES)).T
        for t in range(QUARTERS * QROWS // LANES):
            span = pl.ds(t * LANES, LANES)
            given[slot, :, span] = (turned[slot, :, span] * columns).astype(bf16)
        first = pl.multiple_of(where_from[slot] * ROWS, ROWS)
        copy = pltpu.make_async_copy(given.at[slot], posteriors.at[pl.ds(first, ROWS), :], post_sem.at[slot])
        copy.start()
        post_copies.append(copy)

    per_chunk = [chunk_refs[i * 7:(i + 1) * 7] for i in range(len(CHUNKS))]
    ring_copies = {}
    core_copies, y_copies = {}, {}
    mine_y = core * Y_HIGH

    def product(chunk, q):
        start, wide, counted, _ = chunk
        block = weights[q]
        rows = xbuf[:, :, pl.ds(start, wide)].reshape(GROUP * ROWS, wide)
        value = jnp.dot(block, rows, preferred_element_type=f32)
        if counted:
            ones = jnp.ones((GROUP * ROWS, LANES), bf16)
            value = jnp.concatenate([value, jnp.dot(block, ones, preferred_element_type=f32)], axis=1)
        return value

    def stage_core(j):
        to_core = per_chunk[j][0]
        for yy in range(Y_HIGH):
            to_core[yy] = product(CHUNKS[j], (1 - core) * Y_HIGH + yy).astype(bf16)
        copy = pltpu.make_async_remote_copy(
            src_ref=to_core, dst_ref=per_chunk[j][1], send_sem=core_send.at[j], recv_sem=core_recv.at[j],
            device_id=other_core, device_id_type=MESH)
        copy.start()
        sends.append(copy)
        core_copies[j] = copy

    def ring_start(j, step, up, src, dst):
        d = 0 if up else 1
        copy = pltpu.make_async_remote_copy(
            src_ref=src, dst_ref=dst, send_sem=ring_send.at[j, step, d], recv_sem=ring_recv.at[j, step, d],
            device_id=z_up if up else z_down, device_id_type=MESH)
        copy.start()
        sends.append(copy)
        ring_copies[(j, step, d)] = copy

    def ring_first(j):
        local, out, into = per_chunk[j][2], per_chunk[j][3], per_chunk[j][4]
        rows = local.shape[1]
        mid = rows // 2
        far = (z + 4) % Z_CHIPS
        values = local[far].astype(bf16)
        out[0, 0, 0:mid] = values[0:mid]
        out[0, 1, 0:mid] = values[mid:rows]
        for d in range(2):
            ring_start(j, 0, d == 0, out.at[0, d, pl.ds(0, mid)], into.at[0, d, pl.ds(0, mid)])

    def ring_next(j, step):
        local, out, into = per_chunk[j][2], per_chunk[j][3], per_chunk[j][4]
        rows = local.shape[1]
        mid = rows // 2
        for d in range(2):
            ring_copies[(j, step - 1, d)].wait_recv()
            whose = (z + 4 - step) % Z_CHIPS if d == 0 else (z + 4 + step) % Z_CHIPS
            if step == 1:
                got = into[0, d, 0:mid].astype(f32)
                if d == 0:
                    out[1, d, 0:mid] = (local[whose, 0:mid] + got).astype(bf16)
                    out[1, d, mid:rows] = local[whose, mid:rows].astype(bf16)
                else:
                    out[1, d, 0:mid] = local[whose, 0:mid].astype(bf16)
                    out[1, d, mid:rows] = (local[whose, mid:rows] + got).astype(bf16)
            else:
                out[step, d] = (local[whose] + into[step - 1, d].astype(f32)).astype(bf16)
            ring_start(j, step, d == 0, out.at[step, d], into.at[step, d])

    def ring_sum(j):
        local, into = per_chunk[j][2], per_chunk[j][4]
        for d in range(2):
            ring_copies[(j, 3, d)].wait_recv()
        return local[z] + into[3, 0].astype(f32) + into[3, 1].astype(f32)

    def y_start(j):
        copy = pltpu.make_async_remote_copy(
            src_ref=per_chunk[j][5], dst_ref=per_chunk[j][6], send_sem=y_send.at[j], recv_sem=y_recv.at[j],
            device_id=y_far, device_id_type=MESH)
        copy.start()
        sends.append(copy)
        y_copies[j] = copy

    def stage_local(j):
        from_core, local = per_chunk[j][1], per_chunk[j][2]
        wide = width_of(CHUNKS[j])
        z_first = CHUNKS[j][3] == "z"

        def own(yy):
            value = product(CHUNKS[j], mine_y + yy) + from_core[yy].astype(f32)
            return value.reshape(Z_CHIPS, PER, wide)

        core_copies[j].wait_recv()
        if z_first:
            for yy in range(Y_HIGH):
                local[:, pl.ds(yy * PER, PER), :] = own(yy)
            ring_first(j)
        else:
            per_chunk[j][5][...] = own(1 - y_hi).astype(bf16)
            local[...] = own(y_hi)
            y_start(j)

    state["divide"] = None
    waiting = []

    def finish(j, value):
        start, wide, counted, _ = CHUNKS[j]
        if counted:
            state["divide"] = value[:, wide:wide + LANES] + prior_weight
        prior = table[mine_y + y_hi, z, :, pl.ds(start, wide)].astype(f32)
        references[:, pl.ds(start, wide)] = value[:, 0:wide] + prior_weight * prior
        waiting.append((start, wide))
        if state["divide"] is not None:
            for first, columns in waiting:
                below = jnp.concatenate([state["divide"]] * (columns // LANES), axis=1)
                references[:, pl.ds(first, columns)] = references[:, pl.ds(first, columns)] / below
            waiting.clear()

    def stages(j):
        if CHUNKS[j][3] == "z":
            def to_y():
                local = per_chunk[j][2]
                local[z] = ring_sum(j)
                per_chunk[j][5][...] = local[z, pl.ds(pl.multiple_of((1 - y_hi) * PER, PER), PER), :].astype(bf16)
                y_start(j)

            def last():
                y_copies[j].wait_recv()
                mine = per_chunk[j][2][z, pl.ds(pl.multiple_of(y_hi * PER, PER), PER), :]
                finish(j, mine + per_chunk[j][6][...].astype(f32))

            return [lambda: stage_core(j), lambda: stage_local(j), lambda: ring_next(j, 1), lambda: ring_next(j, 2),
                    lambda: ring_next(j, 3), to_y, last]

        def add_y():
            y_copies[j].wait_recv()
            local = per_chunk[j][2]
            local[...] = local[...] + per_chunk[j][6][...].astype(f32)
            ring_first(j)

        return [lambda: stage_core(j), lambda: stage_local(j), add_y, lambda: ring_next(j, 1), lambda: ring_next(j, 2),
                lambda: ring_next(j, 3), lambda: finish(j, ring_sum(j))]

    plans = [stages(j) for j in range(len(CHUNKS))]
    for place, (j, s) in enumerate(ORDER):
        plans[j][s]()
        if place % 4 == 3 and place // 4 < GROUP:
            give_posteriors(place // 4)

    for copy in sends:
        copy.wait_send()
    for copy in post_copies:
        copy.wait()


def scratch():
    shapes = [
        pltpu.VMEM((GROUP, ROWS), f32),
        pltpu.SMEM((GROUP, Z_CHIPS), jnp.int32),
        pltpu.VMEM((ROWS, DEPTH), f32),
        pltpu.VMEM((GROUP, ROWS, DEPTH), bf16),
        pltpu.VMEM((QUARTERS, Z_CHIPS, PER, DEPTH), bf16),
        pltpu.VMEM((QUARTERS, QROWS, LANES), f32),
        pltpu.VMEM((QROWS, 2 * LANES), f32),
        pltpu.VMEM((QUARTERS, QROWS, GROUP * ROWS), f32),
        pltpu.VMEM((QUARTERS, QROWS, GROUP * ROWS), bf16),
        pltpu.VMEM((GROUP, ROWS, QUARTERS * QROWS), f32),
        pltpu.VMEM((GROUP, ROWS, QUARTERS * QROWS), bf16),
        pltpu.VMEM((2 * GROUP, LANES), f32),
        pltpu.VMEM((GROUP, 2 * GROUP, LANES), f32),
        pltpu.SemaphoreType.DMA((PIECES + 2 + QUARTERS,)),
        pltpu.SemaphoreType.DMA((7 * PIECES,)),
        pltpu.SemaphoreType.DMA((GROUP, PIECES)),
        pltpu.SemaphoreType.DMA((GROUP,)),
        pltpu.SemaphoreType.DMA((GROUP,)),
        pltpu.SemaphoreType.DMA((GROUP,)),
        pltpu.SemaphoreType.DMA((len(CHUNKS),)),
        pltpu.SemaphoreType.DMA((len(CHUNKS),)),
        pltpu.SemaphoreType.DMA((len(CHUNKS), 4, 2)),
        pltpu.SemaphoreType.DMA((len(CHUNKS), 4, 2)),
        pltpu.SemaphoreType.DMA((len(CHUNKS),)),
        pltpu.SemaphoreType.DMA((len(CHUNKS),)),
    ]
    for chunk in CHUNKS:
        wide = width_of(chunk)
        z_first = chunk[3] == "z"
        rows = Y_HIGH * PER if z_first else PER
        y_shape = (PER, wide) if z_first else (Z_CHIPS, PER, wide)
        shapes += [
            pltpu.VMEM((Y_HIGH, QROWS, wide), bf16),
            pltpu.VMEM((Y_HIGH, QROWS, wide), bf16),
            pltpu.VMEM((Z_CHIPS, rows, wide), f32),
            pltpu.VMEM((4, 2, rows, wide), bf16),
            pltpu.VMEM((4, 2, rows, wide), bf16),
            pltpu.VMEM(y_shape, bf16),
            pltpu.VMEM(y_shape, bf16),
        ]
    return shapes


def hand_over(posts, refs, posts_out, refs_out, sem):
    rows = GROUP * ROWS // HANDS
    spans = [pl.ds(i * rows, rows) for i in range(HANDS)]
    copies = [pltpu.make_async_copy(posts.at[s], posts_out.at[s], sem.at[i]) for i, s in enumerate(spans)]
    copies.append(pltpu.make_async_copy(refs, refs_out, sem.at[HANDS]))
    for copy in copies:
        copy.start()
    for copy in copies:
        copy.wait()


def body(images, precision, projections, tile_mask):
    posts, refs = pl.pallas_call(
        kernel,
        out_shape=(
            jax.ShapeDtypeStruct((GROUP * ROWS, QUARTERS * QROWS), bf16),
            jax.ShapeDtypeStruct((PER, DEPTH), f32),
        ),
        in_specs=[
            pl.BlockSpec(memory_space=pltpu.HBM),
            pl.BlockSpec(memory_space=pltpu.HBM),
            pl.BlockSpec(memory_space=pltpu.HBM),
            pl.BlockSpec(memory_space=pltpu.HBM),
        ],
        out_specs=(pl.BlockSpec(memory_space=pl.ANY), pl.BlockSpec(memory_space=pltpu.VMEM)),
        scratch_shapes=scratch(),
        compiler_params=pltpu.CompilerParams(
            collective_id=0, has_side_effects=True, vmem_limit_bytes=40 * 1024 * 1024
        ),
    )(*[pltpu.with_memory_space_constraint(v, pltpu.HBM) for v in (images, precision.reshape(GROUP, ROWS), projections.reshape(Z_CHIPS, Y_HIGH, CORES, PER, DEPTH), tile_mask)])
    return pl.pallas_call(
        hand_over,
        out_shape=(jax.ShapeDtypeStruct(posts.shape, bf16), jax.ShapeDtypeStruct(refs.shape, f32)),
        in_specs=[pl.BlockSpec(memory_space=pl.ANY)] * 2,
        out_specs=(pl.BlockSpec(memory_space=pltpu.HBM), pl.BlockSpec(memory_space=pltpu.HBM)),
        scratch_shapes=[pltpu.SemaphoreType.DMA((HANDS + 1,))],
        compiler_params=pltpu.CompilerParams(vmem_limit_bytes=4 * 1024 * 1024),
    )(posts, refs)


def solution(mesh):
    return jax.shard_map(
        body,
        mesh=mesh,
        in_specs=(P(("img", "ori"), None), P("img"), P("ori", None), P("img", "ori")),
        out_specs=(P("img", "ori"), P(("ori", "img"), None)),
        check_vma=False,
    )
```

```python
import jax
import jax.numpy as jnp
from jax import lax
from jax.experimental import pallas as pl
from jax.experimental.pallas import tpu as pltpu
from jax.sharding import PartitionSpec as P

MESH = pl.DeviceIdType.MESH
prior_weight = 1.0
very_low = -1e30

X_CHIPS, Y_LOW = 4, 2
Z_CHIPS, Y_HIGH, CORES = 8, 2, 2
GROUP = X_CHIPS * Y_LOW
HANDS = 8
ROWS = 128
DEPTH = 2048
PER = 32
QUARTERS = CORES * Y_HIGH
QROWS = Z_CHIPS * PER
LANES = 128
PIECES = 8
STACK = 2
PIECE = DEPTH // PIECES
PIECE_ORDER = (0, 4, 1, 5, 2, 6, 3, 7)
CHUNKS = (
    (0, 256, False, "z"),
    (256, 256, False, "z"),
    (512, 256, False, "y"),
    (768, 256, True, "y"),
    (1024, 256, False, "z"),
    (1280, 256, False, "y"),
    (1536, 256, False, "z"),
    (1792, 256, False, "y"),
)
ORDER = (
    (0, 0), (1, 0), (2, 0), (3, 0), (4, 0), (5, 0), (6, 0), (0, 1), (1, 1), (2, 1), (7, 0), (3, 1),
    (4, 1), (5, 1), (0, 2), (6, 1), (1, 2), (7, 1), (7, 2), (3, 2), (5, 2), (2, 2), (2, 3), (4, 2),
    (3, 3), (0, 3), (6, 2), (1, 3), (5, 3), (2, 4), (7, 3), (4, 3), (3, 4), (0, 4), (6, 3), (1, 4),
    (5, 4), (7, 4), (4, 4), (3, 5), (0, 5), (6, 4), (1, 5), (5, 5), (7, 5), (2, 5), (4, 5), (3, 6),
    (0, 6), (6, 5), (5, 6), (7, 6), (1, 6), (2, 6), (3, 7), (4, 6), (5, 7), (6, 6), (7, 7), (2, 7),
)
STAT_SLOT = {1: 1, 2: 3, 3: 2, 4: 4, 5: 5, 6: 7, 7: 6}

f32 = jnp.float32
bf16 = jnp.bfloat16


def width_of(chunk):
    return chunk[1] + (LANES if chunk[2] else 0)


def kernel(images, precision_hbm, projections, mask_hbm, posteriors, references, precision, tile_mask, raw, xbuf, table, half_squares, bias, lifted,
           weights, turned, given, stat_out, stat_in, load_sem, piece_send, piece_recv, stat_send, stat_recv, post_sem,
           core_send, core_recv, ring_send, ring_recv, y_send, y_recv, *chunk_refs):
    img, ori = lax.axis_index("img"), lax.axis_index("ori")
    z, y_hi, core = img // 4, (img // 2) % 2, img % 2
    x, y_lo = ori // 2, ori % 2

    def at_ori(dx, flip):
        row = 1 - y_lo if flip else y_lo
        return ((x + dx) % X_CHIPS) * 2 + row

    where_from = [at_ori(0, False), at_ori(0, True), at_ori(3, False), at_ori(1, False),
                  at_ori(2, False), at_ori(2, True), at_ori(3, True), at_ori(1, True)]
    peers = [(img, w) for w in where_from]
    y_peer, left, right = peers[1], peers[2], peers[3]
    other_core = (z * 4 + y_hi * 2 + 1 - core, ori)
    z_up = (((z + 1) % Z_CHIPS) * 4 + y_hi * 2 + core, ori)
    z_down = (((z + 7) % Z_CHIPS) * 4 + y_hi * 2 + core, ori)
    y_far = (z * 4 + (1 - y_hi) * 2 + core, ori)

    load_images = []
    for i in PIECE_ORDER:
        span = pl.ds(i * PIECE, PIECE)
        load_images.append(pltpu.make_async_copy(images.at[:, span], raw.at[:, span], load_sem.at[i]))
        load_images[-1].start()
    load_small = [pltpu.make_async_copy(precision_hbm, precision, load_sem.at[PIECES]),
                  pltpu.make_async_copy(mask_hbm, tile_mask, load_sem.at[PIECES + 1])]
    load_table = []
    for c in range(CORES):
        for yy in range(Y_HIGH):
            q = c * Y_HIGH + yy
            load_table.append(
                pltpu.make_async_copy(projections.at[:, yy, c], table.at[q], load_sem.at[PIECES + 2 + q]))

    barrier = pltpu.get_barrier_semaphore()
    friends = peers[1:] + [other_core, z_up, z_down, y_far]
    for friend in friends:
        pl.semaphore_signal(barrier, inc=1, device_id=friend, device_id_type=MESH)

    def lower(place):
        load_images[place].wait()
        span = pl.ds(PIECE_ORDER[place] * PIECE, PIECE)
        xbuf[0, :, span] = raw[:, span].astype(bf16)

    for place in range(2):
        lower(place)
    pl.semaphore_wait(barrier, len(friends))

    sends = []
    arrivals = {}
    counter = [0]

    def send_piece(slot, piece, target, far_slot):
        span = pl.ds(piece * PIECE, PIECE)
        copy = pltpu.make_async_remote_copy(
            src_ref=xbuf.at[slot, :, span], dst_ref=xbuf.at[far_slot, :, span], send_sem=piece_send.at[counter[0]],
            recv_sem=piece_recv.at[far_slot, piece], device_id=target, device_id_type=MESH)
        counter[0] += 1
        copy.start()
        sends.append(copy)
        arrivals[(far_slot, piece)] = copy

    def arrived(slot, piece):
        arrivals[(slot, piece)].wait_recv()

    half = PIECES // 2
    for i in range(half):
        if i > 0:
            lower(2 * i)
            lower(2 * i + 1)
        send_piece(0, i, right, 2)
        send_piece(0, half + i, left, 3)
        send_piece(0, i, y_peer, 1)
        send_piece(0, half + i, y_peer, 1)
    for i in range(half):
        send_piece(0, half + i, right, 2)
        send_piece(0, i, left, 3)

    for copy in load_small + load_table:
        copy.start()
    for copy in load_small + load_table:
        copy.wait()

    def square_tile(q, carry):
        wide = table[q].reshape(QROWS, DEPTH).astype(f32)
        total = jnp.sum(wide * wide, axis=1, keepdims=True)
        half_squares[q] = jnp.broadcast_to(0.5 * total, (QROWS, LANES))
        return carry

    lax.fori_loop(0, QUARTERS, square_tile, 0)

    row_ids = lax.broadcasted_iota(jnp.int32, (GROUP, LANES), 0)
    state = {"high": jnp.zeros((GROUP, LANES), f32), "total": jnp.zeros((GROUP, LANES), f32)}

    def product_tile(q, slots, spans):
        total = None
        for first, last in spans:
            span = pl.ds(first * PIECE, (last - first) * PIECE)
            block = table[q, :, :, span].reshape(QROWS, (last - first) * PIECE)
            rows = xbuf[pl.ds(slots[0], len(slots)), :, span].reshape(len(slots) * ROWS, (last - first) * PIECE)
            part = lax.dot_general(block, rows, (((1,), (1,)), ((), ())), preferred_element_type=f32)
            total = part if total is None else total + part
        return total

    def partial_score(slots, spans):
        cols = pl.ds(slots[0] * LANES, len(slots) * LANES)

        def tile(t, carry):
            for i in range(STACK):
                q = t * STACK + i
                lifted[q, :, cols] = product_tile(q, slots, spans)
            return carry

        lax.fori_loop(0, QUARTERS // STACK, tile, 0)

    def score(slots, spans=((0, PIECES),), started=False):
        wide = len(slots) * LANES
        cols = pl.ds(slots[0] * LANES, wide)
        for k, slot in enumerate(slots):
            for zz in range(Z_CHIPS):
                live = jnp.where(tile_mask[where_from[slot], zz] > 0, 0.0, very_low)
                bias[pl.ds(zz * PER, PER), pl.ds(k * LANES, LANES)] = jnp.full((PER, LANES), live, f32)
        scale = jnp.concatenate([precision[pl.ds(where_from[slot], 1), :] for slot in slots], axis=1)

        def score_tile(t, high):
            for i in range(STACK):
                q = t * STACK + i
                products = product_tile(q, slots, spans)
                if started:
                    products = products + lifted[q, :, cols]
                norm = jnp.concatenate([half_squares[q]] * len(slots), axis=1)
                scores = scale * (products - norm) + bias[:, 0:wide]
                lifted[q, :, cols] = scores
                high = jnp.maximum(high, jnp.max(scores.reshape(QROWS // 8, 8, wide), axis=0))
            return high

        high = lax.fori_loop(0, QUARTERS // STACK, score_tile, jnp.full((8, wide), -3e38, f32))
        high = jnp.max(high, axis=0, keepdims=True)

        def lift_tile(q, total):
            values = jnp.exp(lifted[q, :, cols] - high)
            lifted[q, :, cols] = values
            return total + jnp.sum(values.reshape(QROWS // 8, 8, wide), axis=0)

        total = lax.fori_loop(0, QUARTERS, lift_tile, jnp.zeros((8, wide), f32))
        total = jnp.sum(total, axis=0, keepdims=True)
        for k, slot in enumerate(slots):
            here = row_ids == where_from[slot]
            span = slice(k * LANES, (k + 1) * LANES)
            state["high"] = jnp.where(here, high[:, span], state["high"])
            state["total"] = jnp.where(here, total[:, span], state["total"])

    def turn(slot):
        span = pl.ds(slot * LANES, LANES)

        def tile(zz, carry):
            rows = pl.ds(pl.multiple_of(zz * PER, PER), PER)
            block = jnp.concatenate([lifted[q, rows, span] for q in (0, 2, 1, 3)], axis=0)
            turned[slot, :, pl.ds(pl.multiple_of(zz * LANES, LANES), LANES)] = block.T
            return carry

        lax.fori_loop(0, Z_CHIPS, tile, 0)

    for i in range(half):
        arrived(2, i)
        send_piece(2, i, right, 4)
        arrived(3, half + i)
        send_piece(3, half + i, left, 4)
        if i == 1:
            score((0,))
    for i in range(half):
        arrived(1, i)
        send_piece(1, i, right, 6)
        arrived(1, half + i)
        send_piece(1, half + i, left, 7)
        arrived(2, half + i)
        send_piece(2, half + i, y_peer, 6)
        arrived(3, i)
        send_piece(3, i, y_peer, 7)
        if i == 0:
            turn(0)
    score((1, 2))
    turn(1)
    turn(2)
    for i in range(half):
        arrived(4, i)
        arrived(4, half + i)
    for i in (half - 1, PIECES - 1):
        send_piece(4, i, y_peer, 5)
    for i in range(2):
        arrived(6, half + i)
        send_piece(6, half + i, right, 5)
        arrived(7, i)
        send_piece(7, i, left, 5)
    score((3, 4))
    arrived(6, half + 2)
    send_piece(6, half + 2, right, 5)
    arrived(7, 2)
    send_piece(7, 2, left, 5)
    turn(3)
    turn(4)
    arrived(6, PIECES - 1)
    arrived(7, half - 1)
    for i in range(half):
        arrived(6, i)
        arrived(7, half + i)
    score((6, 7))
    for i in (4, 0, 5, 1, 3):
        arrived(5, i)
    partial_score((5,), ((0, 2), (3, 6)))
    for i in (6, 2, 7):
        arrived(5, i)
    score((5,), ((2, 3), (6, 8)), True)

    my_high, my_total = state["high"], state["total"]
    stat_out[0:GROUP, :] = my_high
    stat_out[GROUP:2 * GROUP, :] = my_total
    stat_copies = []
    for r in range(1, GROUP):
        copy = pltpu.make_async_remote_copy(
            src_ref=stat_out, dst_ref=stat_in.at[STAT_SLOT[r]], send_sem=stat_send.at[r],
            recv_sem=stat_recv.at[STAT_SLOT[r]], device_id=peers[r], device_id_type=MESH)
        copy.start()
        sends.append(copy)
        stat_copies.append(copy)
    for slot in (6, 7, 5):
        turn(slot)
    for copy in stat_copies:
        copy.wait_recv()
    highest = my_high
    for r in range(1, GROUP):
        highest = jnp.maximum(highest, stat_in[r, 0:GROUP, :])
    my_part = jnp.exp(my_high - highest)
    whole = my_total * my_part
    for r in range(1, GROUP):
        whole = whole + stat_in[r, GROUP:2 * GROUP, :] * jnp.exp(stat_in[r, 0:GROUP, :] - highest)
    factor = my_part / whole
    factor_rows = [jnp.sum(jnp.where(row_ids == w, factor, 0.0), axis=0, keepdims=True) for w in where_from]
    factor_row = jnp.concatenate(factor_rows, axis=1)

    def weight_tile(q, carry):
        weights[q] = (lifted[q] * factor_row).astype(bf16)
        return carry

    lax.fori_loop(0, QUARTERS, weight_tile, 0)

    post_copies = []

    def give_posteriors(slot):
        columns = jnp.broadcast_to(factor_rows[slot], (LANES, LANES)).T
        for t in range(QUARTERS * QROWS // LANES):
            span = pl.ds(t * LANES, LANES)
            given[slot, :, span] = (turned[slot, :, span] * columns).astype(bf16)
        first = pl.multiple_of(where_from[slot] * ROWS, ROWS)
        copy = pltpu.make_async_copy(given.at[slot], posteriors.at[pl.ds(first, ROWS), :], post_sem.at[slot])
        copy.start()
        post_copies.append(copy)

    per_chunk = [chunk_refs[i * 7:(i + 1) * 7] for i in range(len(CHUNKS))]
    ring_copies = {}
    core_copies, y_copies = {}, {}
    mine_y = core * Y_HIGH

    def product(chunk, q):
        start, wide, counted, _ = chunk
        block = weights[q]
        rows = xbuf[:, :, pl.ds(start, wide)].reshape(GROUP * ROWS, wide)
        value = jnp.dot(block, rows, preferred_element_type=f32)
        if counted:
            ones = jnp.ones((GROUP * ROWS, LANES), bf16)
            value = jnp.concatenate([value, jnp.dot(block, ones, preferred_element_type=f32)], axis=1)
        return value

    def stage_core(j):
        to_core = per_chunk[j][0]
        for yy in range(Y_HIGH):
            to_core[yy] = product(CHUNKS[j], (1 - core) * Y_HIGH + yy).astype(bf16)
        copy = pltpu.make_async_remote_copy(
            src_ref=to_core, dst_ref=per_chunk[j][1], send_sem=core_send.at[j], recv_sem=core_recv.at[j],
            device_id=other_core, device_id_type=MESH)
        copy.start()
        sends.append(copy)
        core_copies[j] = copy

    def ring_start(j, step, up, src, dst):
        d = 0 if up else 1
        copy = pltpu.make_async_remote_copy(
            src_ref=src, dst_ref=dst, send_sem=ring_send.at[j, step, d], recv_sem=ring_recv.at[j, step, d],
            device_id=z_up if up else z_down, device_id_type=MESH)
        copy.start()
        sends.append(copy)
        ring_copies[(j, step, d)] = copy

    def ring_first(j):
        out, into = per_chunk[j][3], per_chunk[j][4]
        rows = out.shape[2]
        mid = rows // 2
        values = local_rows(j, 4).astype(bf16)
        out[0, 0, 0:mid] = values[0:mid]
        out[0, 1, 0:mid] = values[mid:rows]
        for d in range(2):
            ring_start(j, 0, d == 0, out.at[0, d, pl.ds(0, mid)], into.at[0, d, pl.ds(0, mid)])

    def ring_next(j, step):
        out, into = per_chunk[j][3], per_chunk[j][4]
        rows = out.shape[2]
        mid = rows // 2
        for d in range(2):
            mine = local_rows(j, 4 - step if d == 0 else 4 + step)
            ring_copies[(j, step - 1, d)].wait_recv()
            if step == 1:
                got = into[0, d, 0:mid].astype(f32)
                if d == 0:
                    out[1, d, 0:mid] = (mine[0:mid] + got).astype(bf16)
                    out[1, d, mid:rows] = mine[mid:rows].astype(bf16)
                else:
                    out[1, d, 0:mid] = mine[0:mid].astype(bf16)
                    out[1, d, mid:rows] = (mine[mid:rows] + got).astype(bf16)
            else:
                out[step, d] = (mine + into[step - 1, d].astype(f32)).astype(bf16)
            ring_start(j, step, d == 0, out.at[step, d], into.at[step, d])

    def ring_sum(j):
        into = per_chunk[j][4]
        mine = local_rows(j, 0)
        for d in range(2):
            ring_copies[(j, 3, d)].wait_recv()
        return mine + into[3, 0].astype(f32) + into[3, 1].astype(f32)

    def y_start(j):
        copy = pltpu.make_async_remote_copy(
            src_ref=per_chunk[j][5], dst_ref=per_chunk[j][6], send_sem=y_send.at[j, 0], recv_sem=y_recv.at[j, 0],
            device_id=y_far, device_id_type=MESH)
        copy.start()
        sends.append(copy)
        y_copies[j] = copy

    def y_slices(j, steps):
        for step in steps:
            which = (z + step) % Z_CHIPS
            copy = pltpu.make_async_remote_copy(
                src_ref=per_chunk[j][5].at[which], dst_ref=per_chunk[j][6].at[which], send_sem=y_send.at[j, step],
                recv_sem=y_recv.at[j, step], device_id=y_far, device_id_type=MESH)
            copy.start()
            sends.append(copy)
            y_copies[(j, step)] = copy

    def local_rows(j, step):
        which = (z + step) % Z_CHIPS
        if CHUNKS[j][3] == "z":
            return per_chunk[j][2][which]
        y_copies[(j, step)].wait_recv()
        return per_chunk[j][2][which] + per_chunk[j][6][which].astype(f32)

    def stage_local(j):
        from_core, local = per_chunk[j][1], per_chunk[j][2]
        wide = width_of(CHUNKS[j])
        z_first = CHUNKS[j][3] == "z"

        def own(yy):
            value = product(CHUNKS[j], mine_y + yy) + from_core[yy].astype(f32)
            return value.reshape(Z_CHIPS, PER, wide)

        core_copies[j].wait_recv()
        if z_first:
            for yy in range(Y_HIGH):
                local[:, pl.ds(yy * PER, PER), :] = own(yy)
            ring_first(j)
        else:
            per_chunk[j][5][...] = own(1 - y_hi).astype(bf16)
            local[...] = own(y_hi)
            y_slices(j, (4, 3, 5))

    state["divide"] = None
    waiting = []

    def finish(j, value):
        start, wide, counted, _ = CHUNKS[j]
        if counted:
            state["divide"] = value[:, wide:wide + LANES] + prior_weight
        prior = table[mine_y + y_hi, z, :, pl.ds(start, wide)].astype(f32)
        references[:, pl.ds(start, wide)] = value[:, 0:wide] + prior_weight * prior
        waiting.append((start, wide))
        if state["divide"] is not None:
            for first, columns in waiting:
                below = jnp.concatenate([state["divide"]] * (columns // LANES), axis=1)
                references[:, pl.ds(first, columns)] = references[:, pl.ds(first, columns)] / below
            waiting.clear()

    def stages(j):
        if CHUNKS[j][3] == "z":
            def to_y():
                local = per_chunk[j][2]
                local[z] = ring_sum(j)
                per_chunk[j][5][...] = local[z, pl.ds(pl.multiple_of((1 - y_hi) * PER, PER), PER), :].astype(bf16)
                y_start(j)

            def last():
                y_copies[j].wait_recv()
                mine = per_chunk[j][2][z, pl.ds(pl.multiple_of(y_hi * PER, PER), PER), :]
                finish(j, mine + per_chunk[j][6][...].astype(f32))

            return [lambda: stage_core(j), lambda: stage_local(j), lambda: ring_next(j, 1), lambda: ring_next(j, 2),
                    lambda: ring_next(j, 3), to_y, last]

        return [lambda: stage_core(j), lambda: stage_local(j), lambda: y_slices(j, (2, 6, 1, 7, 0)), lambda: ring_first(j),
                lambda: ring_next(j, 1), lambda: ring_next(j, 2), lambda: ring_next(j, 3), lambda: finish(j, ring_sum(j))]

    plans = [stages(j) for j in range(len(CHUNKS))]
    for place, (j, s) in enumerate(ORDER):
        plans[j][s]()
        if place % 4 == 3 and place // 4 < GROUP:
            give_posteriors(place // 4)

    for copy in sends:
        copy.wait_send()
    for copy in post_copies:
        copy.wait()


def scratch():
    shapes = [
        pltpu.VMEM((GROUP, ROWS), f32),
        pltpu.SMEM((GROUP, Z_CHIPS), jnp.int32),
        pltpu.VMEM((ROWS, DEPTH), f32),
        pltpu.VMEM((GROUP, ROWS, DEPTH), bf16),
        pltpu.VMEM((QUARTERS, Z_CHIPS, PER, DEPTH), bf16),
        pltpu.VMEM((QUARTERS, QROWS, LANES), f32),
        pltpu.VMEM((QROWS, 2 * LANES), f32),
        pltpu.VMEM((QUARTERS, QROWS, GROUP * ROWS), f32),
        pltpu.VMEM((QUARTERS, QROWS, GROUP * ROWS), bf16),
        pltpu.VMEM((GROUP, ROWS, QUARTERS * QROWS), f32),
        pltpu.VMEM((GROUP, ROWS, QUARTERS * QROWS), bf16),
        pltpu.VMEM((2 * GROUP, LANES), f32),
        pltpu.VMEM((GROUP, 2 * GROUP, LANES), f32),
        pltpu.SemaphoreType.DMA((PIECES + 2 + QUARTERS,)),
        pltpu.SemaphoreType.DMA((7 * PIECES,)),
        pltpu.SemaphoreType.DMA((GROUP, PIECES)),
        pltpu.SemaphoreType.DMA((GROUP,)),
        pltpu.SemaphoreType.DMA((GROUP,)),
        pltpu.SemaphoreType.DMA((GROUP,)),
        pltpu.SemaphoreType.DMA((len(CHUNKS),)),
        pltpu.SemaphoreType.DMA((len(CHUNKS),)),
        pltpu.SemaphoreType.DMA((len(CHUNKS), 4, 2)),
        pltpu.SemaphoreType.DMA((len(CHUNKS), 4, 2)),
        pltpu.SemaphoreType.DMA((len(CHUNKS), Z_CHIPS)),
        pltpu.SemaphoreType.DMA((len(CHUNKS), Z_CHIPS)),
    ]
    for chunk in CHUNKS:
        wide = width_of(chunk)
        z_first = chunk[3] == "z"
        rows = Y_HIGH * PER if z_first else PER
        y_shape = (PER, wide) if z_first else (Z_CHIPS, PER, wide)
        shapes += [
            pltpu.VMEM((Y_HIGH, QROWS, wide), bf16),
            pltpu.VMEM((Y_HIGH, QROWS, wide), bf16),
            pltpu.VMEM((Z_CHIPS, rows, wide), f32),
            pltpu.VMEM((4, 2, rows, wide), bf16),
            pltpu.VMEM((4, 2, rows, wide), bf16),
            pltpu.VMEM(y_shape, bf16),
            pltpu.VMEM(y_shape, bf16),
        ]
    return shapes


def hand_over(posts, refs, posts_out, refs_out, sem):
    rows = GROUP * ROWS // HANDS
    spans = [pl.ds(i * rows, rows) for i in range(HANDS)]
    copies = [pltpu.make_async_copy(posts.at[s], posts_out.at[s], sem.at[i]) for i, s in enumerate(spans)]
    copies.append(pltpu.make_async_copy(refs, refs_out, sem.at[HANDS]))
    for copy in copies:
        copy.start()
    for copy in copies:
        copy.wait()


def body(images, precision, projections, tile_mask):
    posts, refs = pl.pallas_call(
        kernel,
        out_shape=(
            jax.ShapeDtypeStruct((GROUP * ROWS, QUARTERS * QROWS), bf16),
            jax.ShapeDtypeStruct((PER, DEPTH), f32),
        ),
        in_specs=[
            pl.BlockSpec(memory_space=pltpu.HBM),
            pl.BlockSpec(memory_space=pltpu.HBM),
            pl.BlockSpec(memory_space=pltpu.HBM),
            pl.BlockSpec(memory_space=pltpu.HBM),
        ],
        out_specs=(pl.BlockSpec(memory_space=pl.ANY), pl.BlockSpec(memory_space=pltpu.VMEM)),
        scratch_shapes=scratch(),
        compiler_params=pltpu.CompilerParams(
            collective_id=0, has_side_effects=True, vmem_limit_bytes=40 * 1024 * 1024
        ),
    )(*[pltpu.with_memory_space_constraint(v, pltpu.HBM) for v in (images, precision.reshape(GROUP, ROWS), projections.reshape(Z_CHIPS, Y_HIGH, CORES, PER, DEPTH), tile_mask)])
    return pl.pallas_call(
        hand_over,
        out_shape=(jax.ShapeDtypeStruct(posts.shape, bf16), jax.ShapeDtypeStruct(refs.shape, f32)),
        in_specs=[pl.BlockSpec(memory_space=pl.ANY)] * 2,
        out_specs=(pl.BlockSpec(memory_space=pltpu.HBM), pl.BlockSpec(memory_space=pltpu.HBM)),
        scratch_shapes=[pltpu.SemaphoreType.DMA((HANDS + 1,))],
        compiler_params=pltpu.CompilerParams(vmem_limit_bytes=4 * 1024 * 1024),
    )(posts, refs)


def solution(mesh):
    return jax.shard_map(
        body,
        mesh=mesh,
        in_specs=(P(("img", "ori"), None), P("img"), P("ori", None), P("img", "ori")),
        out_specs=(P("img", "ori"), P(("ori", "img"), None)),
        check_vma=False,
    )
```

```python
import jax
import jax.numpy as jnp
from jax import lax
from jax.experimental import pallas as pl
from jax.experimental.pallas import tpu as pltpu
from jax.sharding import PartitionSpec as P

MESH = pl.DeviceIdType.MESH
prior_weight = 1.0
very_low = -1e30

X_CHIPS, Y_LOW = 4, 2
Z_CHIPS, Y_HIGH, CORES = 8, 2, 2
GROUP = X_CHIPS * Y_LOW
HANDS = 8
ROWS = 128
DEPTH = 2048
PER = 32
QUARTERS = CORES * Y_HIGH
QROWS = Z_CHIPS * PER
LANES = 128
PIECES = 8
STACK = 2
PIECE = DEPTH // PIECES
PIECE_ORDER = (0, 4, 1, 5, 2, 6, 3, 7)
CHUNKS = (
    (0, 256, False, "z"),
    (256, 256, False, "z"),
    (512, 256, False, "y"),
    (768, 256, True, "y"),
    (1024, 256, False, "z"),
    (1280, 256, False, "y"),
    (1536, 256, False, "z"),
    (1792, 256, False, "y"),
)
ORDER = (
    (0, 0), (1, 0), (2, 0), (3, 0), (4, 0), (5, 0), (6, 0), (0, 1), (1, 1), (2, 1), (7, 0), (3, 1),
    (4, 1), (5, 1), (0, 2), (6, 1), (1, 2), (7, 1), (7, 2), (3, 2), (5, 2), (2, 2), (2, 3), (4, 2),
    (3, 3), (0, 3), (6, 2), (1, 3), (5, 3), (2, 4), (7, 3), (4, 3), (3, 4), (0, 4), (6, 3), (1, 4),
    (5, 4), (7, 4), (4, 4), (3, 5), (0, 5), (6, 4), (1, 5), (5, 5), (7, 5), (2, 5), (4, 5), (3, 6),
    (0, 6), (6, 5), (5, 6), (7, 6), (1, 6), (2, 6), (3, 7), (4, 6), (5, 7), (6, 6), (7, 7), (2, 7),
)
STAT_SLOT = {1: 1, 2: 3, 3: 2, 4: 4, 5: 5, 6: 7, 7: 6}

f32 = jnp.float32
bf16 = jnp.bfloat16


def width_of(chunk):
    return chunk[1] + (LANES if chunk[2] else 0)


def kernel(images, precision_hbm, projections, mask_hbm, posteriors, references, precision, tile_mask, raw, xbuf, table, half_squares, bias, lifted,
           weights, turned, given, stat_out, stat_in, ready, load_sem, piece_send, piece_recv, stat_send, stat_recv, post_sem,
           core_send, core_recv, ring_send, ring_recv, y_send, y_recv, *chunk_refs):
    img, ori = lax.axis_index("img"), lax.axis_index("ori")
    z, y_hi, core = img // 4, (img // 2) % 2, img % 2
    x, y_lo = ori // 2, ori % 2

    def at_ori(dx, flip):
        row = 1 - y_lo if flip else y_lo
        return ((x + dx) % X_CHIPS) * 2 + row

    where_from = [at_ori(0, False), at_ori(0, True), at_ori(3, False), at_ori(1, False),
                  at_ori(2, False), at_ori(2, True), at_ori(3, True), at_ori(1, True)]
    peers = [(img, w) for w in where_from]
    y_peer, left, right = peers[1], peers[2], peers[3]
    other_core = (z * 4 + y_hi * 2 + 1 - core, ori)
    z_up = (((z + 1) % Z_CHIPS) * 4 + y_hi * 2 + core, ori)
    z_down = (((z + 7) % Z_CHIPS) * 4 + y_hi * 2 + core, ori)
    y_far = (z * 4 + (1 - y_hi) * 2 + core, ori)

    load_images = []
    for i in PIECE_ORDER:
        span = pl.ds(i * PIECE, PIECE)
        load_images.append(pltpu.make_async_copy(images.at[:, span], raw.at[:, span], load_sem.at[i]))
        load_images[-1].start()
    load_small = [pltpu.make_async_copy(precision_hbm, precision, load_sem.at[PIECES]),
                  pltpu.make_async_copy(mask_hbm, tile_mask, load_sem.at[PIECES + 1])]
    load_table = []
    for c in range(CORES):
        for yy in range(Y_HIGH):
            q = c * Y_HIGH + yy
            load_table.append(
                pltpu.make_async_copy(projections.at[:, yy, c], table.at[q], load_sem.at[PIECES + 2 + q]))

    barrier = pltpu.get_barrier_semaphore()
    y = y_hi * Y_LOW + y_lo
    y_sides = []
    for step in (1, 3):
        there = (y + step) % (Y_HIGH * Y_LOW)
        y_sides.append((z * 4 + (there // Y_LOW) * 2 + core, x * 2 + there % Y_LOW))
    friends = y_sides + [left, right, other_core, z_up, z_down]
    for friend in friends:
        pl.semaphore_signal(barrier, inc=1, device_id=friend, device_id_type=MESH)

    def lower(place):
        load_images[place].wait()
        span = pl.ds(PIECE_ORDER[place] * PIECE, PIECE)
        xbuf[0, :, span] = raw[:, span].astype(bf16)

    for place in range(2):
        lower(place)
    pl.semaphore_wait(barrier, len(friends))
    for side in y_sides:
        pl.semaphore_signal(ready, inc=1, device_id=side, device_id_type=MESH)

    sends = []
    arrivals = {}
    counter = [0]

    def send_piece(slot, piece, target, far_slot):
        span = pl.ds(piece * PIECE, PIECE)
        copy = pltpu.make_async_remote_copy(
            src_ref=xbuf.at[slot, :, span], dst_ref=xbuf.at[far_slot, :, span], send_sem=piece_send.at[counter[0]],
            recv_sem=piece_recv.at[far_slot, piece], device_id=target, device_id_type=MESH)
        counter[0] += 1
        copy.start()
        sends.append(copy)
        arrivals[(far_slot, piece)] = copy

    def arrived(slot, piece):
        arrivals[(slot, piece)].wait_recv()

    half = PIECES // 2
    for i in range(half):
        if i > 0:
            lower(2 * i)
            lower(2 * i + 1)
        send_piece(0, i, right, 2)
        send_piece(0, half + i, left, 3)
        send_piece(0, i, y_peer, 1)
        send_piece(0, half + i, y_peer, 1)
    for i in range(half):
        send_piece(0, half + i, right, 2)
        send_piece(0, i, left, 3)

    for copy in load_small + load_table:
        copy.start()
    for copy in load_small + load_table:
        copy.wait()

    def square_tile(q, carry):
        wide = table[q].reshape(QROWS, DEPTH).astype(f32)
        total = jnp.sum(wide * wide, axis=1, keepdims=True)
        half_squares[q] = jnp.broadcast_to(0.5 * total, (QROWS, LANES))
        return carry

    lax.fori_loop(0, QUARTERS, square_tile, 0)

    row_ids = lax.broadcasted_iota(jnp.int32, (GROUP, LANES), 0)
    state = {"high": jnp.zeros((GROUP, LANES), f32), "total": jnp.zeros((GROUP, LANES), f32)}

    def product_tile(q, slots, spans):
        total = None
        for first, last in spans:
            span = pl.ds(first * PIECE, (last - first) * PIECE)
            block = table[q, :, :, span].reshape(QROWS, (last - first) * PIECE)
            rows = xbuf[pl.ds(slots[0], len(slots)), :, span].reshape(len(slots) * ROWS, (last - first) * PIECE)
            part = lax.dot_general(block, rows, (((1,), (1,)), ((), ())), preferred_element_type=f32)
            total = part if total is None else total + part
        return total

    def partial_score(slots, spans):
        cols = pl.ds(slots[0] * LANES, len(slots) * LANES)

        def tile(t, carry):
            for i in range(STACK):
                q = t * STACK + i
                lifted[q, :, cols] = product_tile(q, slots, spans)
            return carry

        lax.fori_loop(0, QUARTERS // STACK, tile, 0)

    def score(slots, spans=((0, PIECES),), started=False):
        wide = len(slots) * LANES
        cols = pl.ds(slots[0] * LANES, wide)
        for k, slot in enumerate(slots):
            for zz in range(Z_CHIPS):
                live = jnp.where(tile_mask[where_from[slot], zz] > 0, 0.0, very_low)
                bias[pl.ds(zz * PER, PER), pl.ds(k * LANES, LANES)] = jnp.full((PER, LANES), live, f32)
        scale = jnp.concatenate([precision[pl.ds(where_from[slot], 1), :] for slot in slots], axis=1)

        def score_tile(t, high):
            for i in range(STACK):
                q = t * STACK + i
                products = product_tile(q, slots, spans)
                if started:
                    products = products + lifted[q, :, cols]
                norm = jnp.concatenate([half_squares[q]] * len(slots), axis=1)
                scores = scale * (products - norm) + bias[:, 0:wide]
                lifted[q, :, cols] = scores
                high = jnp.maximum(high, jnp.max(scores.reshape(QROWS // 8, 8, wide), axis=0))
            return high

        high = lax.fori_loop(0, QUARTERS // STACK, score_tile, jnp.full((8, wide), -3e38, f32))
        high = jnp.max(high, axis=0, keepdims=True)

        def lift_tile(q, total):
            values = jnp.exp(lifted[q, :, cols] - high)
            lifted[q, :, cols] = values
            return total + jnp.sum(values.reshape(QROWS // 8, 8, wide), axis=0)

        total = lax.fori_loop(0, QUARTERS, lift_tile, jnp.zeros((8, wide), f32))
        total = jnp.sum(total, axis=0, keepdims=True)
        for k, slot in enumerate(slots):
            here = row_ids == where_from[slot]
            span = slice(k * LANES, (k + 1) * LANES)
            state["high"] = jnp.where(here, high[:, span], state["high"])
            state["total"] = jnp.where(here, total[:, span], state["total"])

    def turn(slot):
        span = pl.ds(slot * LANES, LANES)

        def tile(zz, carry):
            rows = pl.ds(pl.multiple_of(zz * PER, PER), PER)
            block = jnp.concatenate([lifted[q, rows, span] for q in (0, 2, 1, 3)], axis=0)
            turned[slot, :, pl.ds(pl.multiple_of(zz * LANES, LANES), LANES)] = block.T
            return carry

        lax.fori_loop(0, Z_CHIPS, tile, 0)

    for i in range(half):
        arrived(2, i)
        send_piece(2, i, right, 4)
        arrived(3, half + i)
        send_piece(3, half + i, left, 4)
        if i == 1:
            score((0,))
    for i in range(half):
        arrived(1, i)
        send_piece(1, i, right, 6)
        arrived(1, half + i)
        send_piece(1, half + i, left, 7)
        arrived(2, half + i)
        send_piece(2, half + i, y_peer, 6)
        arrived(3, i)
        send_piece(3, i, y_peer, 7)
        if i == 0:
            turn(0)
    score((1, 2))
    turn(1)
    turn(2)
    for i in range(half):
        arrived(4, i)
        arrived(4, half + i)
    for i in (half - 1, PIECES - 1):
        send_piece(4, i, y_peer, 5)
    for i in range(2):
        arrived(6, half + i)
        send_piece(6, half + i, right, 5)
        arrived(7, i)
        send_piece(7, i, left, 5)
    score((3, 4))
    arrived(6, half + 2)
    send_piece(6, half + 2, right, 5)
    arrived(7, 2)
    send_piece(7, 2, left, 5)
    turn(3)
    turn(4)
    arrived(6, PIECES - 1)
    arrived(7, half - 1)
    for i in range(half):
        arrived(6, i)
        arrived(7, half + i)
    score((6, 7))
    for i in (4, 0, 5, 1, 3):
        arrived(5, i)
    partial_score((5,), ((0, 2), (3, 6)))
    for i in (6, 2, 7):
        arrived(5, i)
    score((5,), ((2, 3), (6, 8)), True)

    my_high, my_total = state["high"], state["total"]
    stat_out[0:GROUP, :] = my_high
    stat_out[GROUP:2 * GROUP, :] = my_total
    stat_copies = []
    for r in range(1, GROUP):
        copy = pltpu.make_async_remote_copy(
            src_ref=stat_out, dst_ref=stat_in.at[STAT_SLOT[r]], send_sem=stat_send.at[r],
            recv_sem=stat_recv.at[STAT_SLOT[r]], device_id=peers[r], device_id_type=MESH)
        copy.start()
        sends.append(copy)
        stat_copies.append(copy)
    for slot in (6, 7, 5):
        turn(slot)
    for copy in stat_copies:
        copy.wait_recv()
    highest = my_high
    for r in range(1, GROUP):
        highest = jnp.maximum(highest, stat_in[r, 0:GROUP, :])
    my_part = jnp.exp(my_high - highest)
    whole = my_total * my_part
    for r in range(1, GROUP):
        whole = whole + stat_in[r, GROUP:2 * GROUP, :] * jnp.exp(stat_in[r, 0:GROUP, :] - highest)
    factor = my_part / whole
    factor_rows = [jnp.sum(jnp.where(row_ids == w, factor, 0.0), axis=0, keepdims=True) for w in where_from]
    factor_row = jnp.concatenate(factor_rows, axis=1)

    def weight_tile(q, carry):
        weights[q] = (lifted[q] * factor_row).astype(bf16)
        return carry

    lax.fori_loop(0, QUARTERS, weight_tile, 0)

    post_copies = []

    def give_posteriors(slot):
        columns = jnp.broadcast_to(factor_rows[slot], (LANES, LANES)).T
        for t in range(QUARTERS * QROWS // LANES):
            span = pl.ds(t * LANES, LANES)
            given[slot, :, span] = (turned[slot, :, span] * columns).astype(bf16)
        first = pl.multiple_of(where_from[slot] * ROWS, ROWS)
        copy = pltpu.make_async_copy(given.at[slot], posteriors.at[pl.ds(first, ROWS), :], post_sem.at[slot])
        copy.start()
        post_copies.append(copy)

    per_chunk = [chunk_refs[i * 7:(i + 1) * 7] for i in range(len(CHUNKS))]
    ring_copies = {}
    core_copies, y_copies = {}, {}
    mine_y = core * Y_HIGH

    def product(chunk, q):
        start, wide, counted, _ = chunk
        block = weights[q]
        rows = xbuf[:, :, pl.ds(start, wide)].reshape(GROUP * ROWS, wide)
        value = jnp.dot(block, rows, preferred_element_type=f32)
        if counted:
            ones = jnp.ones((GROUP * ROWS, LANES), bf16)
            value = jnp.concatenate([value, jnp.dot(block, ones, preferred_element_type=f32)], axis=1)
        return value

    def stage_core(j):
        to_core = per_chunk[j][0]
        for yy in range(Y_HIGH):
            to_core[yy] = product(CHUNKS[j], (1 - core) * Y_HIGH + yy).astype(bf16)
        copy = pltpu.make_async_remote_copy(
            src_ref=to_core, dst_ref=per_chunk[j][1], send_sem=core_send.at[j], recv_sem=core_recv.at[j],
            device_id=other_core, device_id_type=MESH)
        copy.start()
        sends.append(copy)
        core_copies[j] = copy

    def ring_start(j, step, up, src, dst):
        d = 0 if up else 1
        copy = pltpu.make_async_remote_copy(
            src_ref=src, dst_ref=dst, send_sem=ring_send.at[j, step, d], recv_sem=ring_recv.at[j, step, d],
            device_id=z_up if up else z_down, device_id_type=MESH)
        copy.start()
        sends.append(copy)
        ring_copies[(j, step, d)] = copy

    def ring_first(j):
        out, into = per_chunk[j][3], per_chunk[j][4]
        rows = out.shape[2]
        mid = rows // 2
        values = local_rows(j, 4).astype(bf16)
        out[0, 0, 0:mid] = values[0:mid]
        out[0, 1, 0:mid] = values[mid:rows]
        for d in range(2):
            ring_start(j, 0, d == 0, out.at[0, d, pl.ds(0, mid)], into.at[0, d, pl.ds(0, mid)])

    def ring_next(j, step):
        out, into = per_chunk[j][3], per_chunk[j][4]
        rows = out.shape[2]
        mid = rows // 2
        for d in range(2):
            mine = local_rows(j, 4 - step if d == 0 else 4 + step)
            ring_copies[(j, step - 1, d)].wait_recv()
            if step == 1:
                got = into[0, d, 0:mid].astype(f32)
                if d == 0:
                    out[1, d, 0:mid] = (mine[0:mid] + got).astype(bf16)
                    out[1, d, mid:rows] = mine[mid:rows].astype(bf16)
                else:
                    out[1, d, 0:mid] = mine[0:mid].astype(bf16)
                    out[1, d, mid:rows] = (mine[mid:rows] + got).astype(bf16)
            else:
                out[step, d] = (mine + into[step - 1, d].astype(f32)).astype(bf16)
            ring_start(j, step, d == 0, out.at[step, d], into.at[step, d])

    def ring_sum(j):
        into = per_chunk[j][4]
        mine = local_rows(j, 0)
        for d in range(2):
            ring_copies[(j, 3, d)].wait_recv()
        return mine + into[3, 0].astype(f32) + into[3, 1].astype(f32)

    def y_start(j):
        copy = pltpu.make_async_remote_copy(
            src_ref=per_chunk[j][5], dst_ref=per_chunk[j][6], send_sem=y_send.at[j, 0], recv_sem=y_recv.at[j, 0],
            device_id=y_far, device_id_type=MESH)
        copy.start()
        sends.append(copy)
        y_copies[j] = copy

    def y_slices(j, steps):
        for step in steps:
            which = (z + step) % Z_CHIPS
            copy = pltpu.make_async_remote_copy(
                src_ref=per_chunk[j][5].at[which], dst_ref=per_chunk[j][6].at[which], send_sem=y_send.at[j, step],
                recv_sem=y_recv.at[j, step], device_id=y_far, device_id_type=MESH)
            copy.start()
            sends.append(copy)
            y_copies[(j, step)] = copy

    def local_rows(j, step):
        which = (z + step) % Z_CHIPS
        if CHUNKS[j][3] == "z":
            return per_chunk[j][2][which]
        y_copies[(j, step)].wait_recv()
        return per_chunk[j][2][which] + per_chunk[j][6][which].astype(f32)

    def stage_local(j):
        from_core, local = per_chunk[j][1], per_chunk[j][2]
        wide = width_of(CHUNKS[j])
        z_first = CHUNKS[j][3] == "z"

        def own(yy):
            value = product(CHUNKS[j], mine_y + yy) + from_core[yy].astype(f32)
            return value.reshape(Z_CHIPS, PER, wide)

        core_copies[j].wait_recv()
        if z_first:
            for yy in range(Y_HIGH):
                local[:, pl.ds(yy * PER, PER), :] = own(yy)
            ring_first(j)
        else:
            per_chunk[j][5][...] = own(1 - y_hi).astype(bf16)
            local[...] = own(y_hi)
            y_slices(j, (4, 3, 5))

    state["divide"] = None
    waiting = []

    def finish(j, value):
        start, wide, counted, _ = CHUNKS[j]
        if counted:
            state["divide"] = value[:, wide:wide + LANES] + prior_weight
        prior = table[mine_y + y_hi, z, :, pl.ds(start, wide)].astype(f32)
        references[:, pl.ds(start, wide)] = value[:, 0:wide] + prior_weight * prior
        waiting.append((start, wide))
        if state["divide"] is not None:
            for first, columns in waiting:
                below = jnp.concatenate([state["divide"]] * (columns // LANES), axis=1)
                references[:, pl.ds(first, columns)] = references[:, pl.ds(first, columns)] / below
            waiting.clear()

    def stages(j):
        if CHUNKS[j][3] == "z":
            def to_y():
                local = per_chunk[j][2]
                local[z] = ring_sum(j)
                per_chunk[j][5][...] = local[z, pl.ds(pl.multiple_of((1 - y_hi) * PER, PER), PER), :].astype(bf16)
                y_start(j)

            def last():
                y_copies[j].wait_recv()
                mine = per_chunk[j][2][z, pl.ds(pl.multiple_of(y_hi * PER, PER), PER), :]
                finish(j, mine + per_chunk[j][6][...].astype(f32))

            return [lambda: stage_core(j), lambda: stage_local(j), lambda: ring_next(j, 1), lambda: ring_next(j, 2),
                    lambda: ring_next(j, 3), to_y, last]

        return [lambda: stage_core(j), lambda: stage_local(j), lambda: y_slices(j, (2, 6, 1, 7, 0)), lambda: ring_first(j),
                lambda: ring_next(j, 1), lambda: ring_next(j, 2), lambda: ring_next(j, 3), lambda: finish(j, ring_sum(j))]

    pl.semaphore_wait(ready, 2)
    plans = [stages(j) for j in range(len(CHUNKS))]
    for place, (j, s) in enumerate(ORDER):
        plans[j][s]()
        if place % 4 == 3 and place // 4 < GROUP:
            give_posteriors(place // 4)

    for copy in sends:
        copy.wait_send()
    for copy in post_copies:
        copy.wait()


def scratch():
    shapes = [
        pltpu.VMEM((GROUP, ROWS), f32),
        pltpu.SMEM((GROUP, Z_CHIPS), jnp.int32),
        pltpu.VMEM((ROWS, DEPTH), f32),
        pltpu.VMEM((GROUP, ROWS, DEPTH), bf16),
        pltpu.VMEM((QUARTERS, Z_CHIPS, PER, DEPTH), bf16),
        pltpu.VMEM((QUARTERS, QROWS, LANES), f32),
        pltpu.VMEM((QROWS, 2 * LANES), f32),
        pltpu.VMEM((QUARTERS, QROWS, GROUP * ROWS), f32),
        pltpu.VMEM((QUARTERS, QROWS, GROUP * ROWS), bf16),
        pltpu.VMEM((GROUP, ROWS, QUARTERS * QROWS), f32),
        pltpu.VMEM((GROUP, ROWS, QUARTERS * QROWS), bf16),
        pltpu.VMEM((2 * GROUP, LANES), f32),
        pltpu.VMEM((GROUP, 2 * GROUP, LANES), f32),
        pltpu.SemaphoreType.REGULAR,
        pltpu.SemaphoreType.DMA((PIECES + 2 + QUARTERS,)),
        pltpu.SemaphoreType.DMA((7 * PIECES,)),
        pltpu.SemaphoreType.DMA((GROUP, PIECES)),
        pltpu.SemaphoreType.DMA((GROUP,)),
        pltpu.SemaphoreType.DMA((GROUP,)),
        pltpu.SemaphoreType.DMA((GROUP,)),
        pltpu.SemaphoreType.DMA((len(CHUNKS),)),
        pltpu.SemaphoreType.DMA((len(CHUNKS),)),
        pltpu.SemaphoreType.DMA((len(CHUNKS), 4, 2)),
        pltpu.SemaphoreType.DMA((len(CHUNKS), 4, 2)),
        pltpu.SemaphoreType.DMA((len(CHUNKS), Z_CHIPS)),
        pltpu.SemaphoreType.DMA((len(CHUNKS), Z_CHIPS)),
    ]
    for chunk in CHUNKS:
        wide = width_of(chunk)
        z_first = chunk[3] == "z"
        rows = Y_HIGH * PER if z_first else PER
        y_shape = (PER, wide) if z_first else (Z_CHIPS, PER, wide)
        shapes += [
            pltpu.VMEM((Y_HIGH, QROWS, wide), bf16),
            pltpu.VMEM((Y_HIGH, QROWS, wide), bf16),
            pltpu.VMEM((Z_CHIPS, rows, wide), f32),
            pltpu.VMEM((4, 2, rows, wide), bf16),
            pltpu.VMEM((4, 2, rows, wide), bf16),
            pltpu.VMEM(y_shape, bf16),
            pltpu.VMEM(y_shape, bf16),
        ]
    return shapes


def hand_over(posts, refs, posts_out, refs_out, sem):
    rows = GROUP * ROWS // HANDS
    spans = [pl.ds(i * rows, rows) for i in range(HANDS)]
    copies = [pltpu.make_async_copy(posts.at[s], posts_out.at[s], sem.at[i]) for i, s in enumerate(spans)]
    copies.append(pltpu.make_async_copy(refs, refs_out, sem.at[HANDS]))
    for copy in copies:
        copy.start()
    for copy in copies:
        copy.wait()


def body(images, precision, projections, tile_mask):
    posts, refs = pl.pallas_call(
        kernel,
        out_shape=(
            jax.ShapeDtypeStruct((GROUP * ROWS, QUARTERS * QROWS), bf16),
            jax.ShapeDtypeStruct((PER, DEPTH), f32),
        ),
        in_specs=[
            pl.BlockSpec(memory_space=pltpu.HBM),
            pl.BlockSpec(memory_space=pltpu.HBM),
            pl.BlockSpec(memory_space=pltpu.HBM),
            pl.BlockSpec(memory_space=pltpu.HBM),
        ],
        out_specs=(pl.BlockSpec(memory_space=pl.ANY), pl.BlockSpec(memory_space=pltpu.VMEM)),
        scratch_shapes=scratch(),
        compiler_params=pltpu.CompilerParams(
            collective_id=0, has_side_effects=True, vmem_limit_bytes=40 * 1024 * 1024
        ),
    )(*[pltpu.with_memory_space_constraint(v, pltpu.HBM) for v in (images, precision.reshape(GROUP, ROWS), projections.reshape(Z_CHIPS, Y_HIGH, CORES, PER, DEPTH), tile_mask)])
    return pl.pallas_call(
        hand_over,
        out_shape=(jax.ShapeDtypeStruct(posts.shape, bf16), jax.ShapeDtypeStruct(refs.shape, f32)),
        in_specs=[pl.BlockSpec(memory_space=pl.ANY)] * 2,
        out_specs=(pl.BlockSpec(memory_space=pltpu.HBM), pl.BlockSpec(memory_space=pltpu.HBM)),
        scratch_shapes=[pltpu.SemaphoreType.DMA((HANDS + 1,))],
        compiler_params=pltpu.CompilerParams(vmem_limit_bytes=4 * 1024 * 1024),
    )(posts, refs)


def solution(mesh):
    return jax.shard_map(
        body,
        mesh=mesh,
        in_specs=(P(("img", "ori"), None), P("img"), P("ori", None), P("img", "ori")),
        out_specs=(P("img", "ori"), P(("ori", "img"), None)),
        check_vma=False,
    )
```

```python
import jax
import jax.numpy as jnp
from jax import lax
from jax.experimental import pallas as pl
from jax.experimental.pallas import tpu as pltpu
from jax.sharding import PartitionSpec as P

MESH = pl.DeviceIdType.MESH
prior_weight = 1.0
very_low = -1e30

X_CHIPS, Y_LOW = 4, 2
Z_CHIPS, Y_HIGH, CORES = 8, 2, 2
GROUP = X_CHIPS * Y_LOW
HANDS = 8
ROWS = 128
DEPTH = 2048
PER = 32
QUARTERS = CORES * Y_HIGH
QROWS = Z_CHIPS * PER
LANES = 128
PIECES = 8
STACK = 2
PIECE = DEPTH // PIECES
PIECE_ORDER = (0, 4, 1, 5, 2, 6, 3, 7)
CHUNKS = (
    (0, 256, False, "z"),
    (256, 256, False, "z"),
    (512, 256, False, "y"),
    (768, 256, True, "y"),
    (1024, 256, False, "z"),
    (1280, 256, False, "y"),
    (1536, 256, False, "z"),
    (1792, 256, False, "y"),
)
ORDER = (
    (0, 0), (1, 0), (2, 0), (3, 0), (4, 0), (5, 0), (6, 0), (0, 1), (1, 1), (2, 1), (7, 0), (3, 1),
    (4, 1), (5, 1), (0, 2), (6, 1), (1, 2), (7, 1), (7, 2), (3, 2), (5, 2), (2, 2), (2, 3), (4, 2),
    (3, 3), (0, 3), (6, 2), (1, 3), (5, 3), (2, 4), (7, 3), (4, 3), (3, 4), (0, 4), (6, 3), (1, 4),
    (5, 4), (7, 4), (4, 4), (3, 5), (0, 5), (6, 4), (1, 5), (5, 5), (7, 5), (2, 5), (4, 5), (3, 6),
    (0, 6), (6, 5), (5, 6), (7, 6), (1, 6), (2, 6), (3, 7), (4, 6), (5, 7), (6, 6), (7, 7), (2, 7),
)
STAT_SLOT = {1: 1, 2: 3, 3: 2, 4: 4, 5: 5, 6: 7, 7: 6}

f32 = jnp.float32
bf16 = jnp.bfloat16


def width_of(chunk):
    return chunk[1] + (LANES if chunk[2] else 0)


def kernel(images, precision_hbm, projections, mask_hbm, posteriors, references, precision, tile_mask, raw, xbuf, table, half_squares, bias, lifted,
           weights, turned, given, stat_out, stat_in, ready, load_sem, piece_send, piece_recv, stat_send, stat_recv, post_sem,
           core_send, core_recv, ring_send, ring_recv, y_send, y_recv, *chunk_refs):
    img, ori = lax.axis_index("img"), lax.axis_index("ori")
    z, y_hi, core = img // 4, (img // 2) % 2, img % 2
    x, y_lo = ori // 2, ori % 2

    def at_ori(dx, flip):
        row = 1 - y_lo if flip else y_lo
        return ((x + dx) % X_CHIPS) * 2 + row

    where_from = [at_ori(0, False), at_ori(0, True), at_ori(3, False), at_ori(1, False),
                  at_ori(2, False), at_ori(2, True), at_ori(3, True), at_ori(1, True)]
    peers = [(img, w) for w in where_from]
    y_peer, left, right = peers[1], peers[2], peers[3]
    other_core = (z * 4 + y_hi * 2 + 1 - core, ori)
    z_up = (((z + 1) % Z_CHIPS) * 4 + y_hi * 2 + core, ori)
    z_down = (((z + 7) % Z_CHIPS) * 4 + y_hi * 2 + core, ori)
    y_far = (z * 4 + (1 - y_hi) * 2 + core, ori)

    load_images = []
    for i in PIECE_ORDER:
        span = pl.ds(i * PIECE, PIECE)
        load_images.append(pltpu.make_async_copy(images.at[:, span], raw.at[:, span], load_sem.at[i]))
        load_images[-1].start()
    load_small = [pltpu.make_async_copy(precision_hbm, precision, load_sem.at[PIECES]),
                  pltpu.make_async_copy(mask_hbm, tile_mask, load_sem.at[PIECES + 1])]
    load_table = []
    for c in range(CORES):
        for yy in range(Y_HIGH):
            q = c * Y_HIGH + yy
            load_table.append(
                pltpu.make_async_copy(projections.at[:, yy, c], table.at[q], load_sem.at[PIECES + 2 + q]))

    barrier = pltpu.get_barrier_semaphore()
    y = y_hi * Y_LOW + y_lo
    y_sides = []
    for step in (1, 3):
        there = (y + step) % (Y_HIGH * Y_LOW)
        y_sides.append((z * 4 + (there // Y_LOW) * 2 + core, x * 2 + there % Y_LOW))
    friends = y_sides + [left, right, other_core, z_up, z_down]
    for friend in friends:
        pl.semaphore_signal(barrier, inc=1, device_id=friend, device_id_type=MESH)

    def lower(place):
        load_images[place].wait()
        span = pl.ds(PIECE_ORDER[place] * PIECE, PIECE)
        xbuf[0, :, span] = raw[:, span].astype(bf16)

    for place in range(2):
        lower(place)
    pl.semaphore_wait(barrier, len(friends))
    for side in y_sides:
        pl.semaphore_signal(ready, inc=1, device_id=side, device_id_type=MESH)

    sends = []
    arrivals = {}
    counter = [0]

    def send_piece(slot, piece, target, far_slot):
        span = pl.ds(piece * PIECE, PIECE)
        copy = pltpu.make_async_remote_copy(
            src_ref=xbuf.at[slot, :, span], dst_ref=xbuf.at[far_slot, :, span], send_sem=piece_send.at[counter[0]],
            recv_sem=piece_recv.at[far_slot, piece], device_id=target, device_id_type=MESH)
        counter[0] += 1
        copy.start()
        sends.append(copy)
        arrivals[(far_slot, piece)] = copy

    def arrived(slot, piece):
        arrivals[(slot, piece)].wait_recv()

    half = PIECES // 2
    for i in range(half):
        if i > 0:
            lower(2 * i)
            lower(2 * i + 1)
        send_piece(0, i, right, 2)
        send_piece(0, half + i, left, 3)
        send_piece(0, i, y_peer, 1)
        send_piece(0, half + i, y_peer, 1)
    for i in range(half):
        send_piece(0, half + i, right, 2)
        send_piece(0, i, left, 3)

    for copy in load_small + load_table:
        copy.start()
    for copy in load_small + load_table:
        copy.wait()

    def square_tile(q, carry):
        wide = table[q].reshape(QROWS, DEPTH).astype(f32)
        total = jnp.sum(wide * wide, axis=1, keepdims=True)
        half_squares[q] = jnp.broadcast_to(0.5 * total, (QROWS, LANES))
        return carry

    lax.fori_loop(0, QUARTERS, square_tile, 0)

    row_ids = lax.broadcasted_iota(jnp.int32, (GROUP, LANES), 0)
    state = {"high": jnp.zeros((GROUP, LANES), f32), "total": jnp.zeros((GROUP, LANES), f32)}

    def product_tile(q, slots, spans):
        total = None
        for first, last in spans:
            span = pl.ds(first * PIECE, (last - first) * PIECE)
            block = table[q, :, :, span].reshape(QROWS, (last - first) * PIECE)
            rows = xbuf[pl.ds(slots[0], len(slots)), :, span].reshape(len(slots) * ROWS, (last - first) * PIECE)
            part = lax.dot_general(block, rows, (((1,), (1,)), ((), ())), preferred_element_type=f32)
            total = part if total is None else total + part
        return total

    def partial_score(slots, spans):
        cols = pl.ds(slots[0] * LANES, len(slots) * LANES)

        def tile(t, carry):
            for i in range(STACK):
                q = t * STACK + i
                lifted[q, :, cols] = product_tile(q, slots, spans)
            return carry

        lax.fori_loop(0, QUARTERS // STACK, tile, 0)

    def score(slots, spans=((0, PIECES),), started=False):
        wide = len(slots) * LANES
        cols = pl.ds(slots[0] * LANES, wide)
        for k, slot in enumerate(slots):
            for zz in range(Z_CHIPS):
                live = jnp.where(tile_mask[where_from[slot], zz] > 0, 0.0, very_low)
                bias[pl.ds(zz * PER, PER), pl.ds(k * LANES, LANES)] = jnp.full((PER, LANES), live, f32)
        scale = jnp.concatenate([precision[pl.ds(where_from[slot], 1), :] for slot in slots], axis=1)

        def score_tile(t, high):
            for i in range(STACK):
                q = t * STACK + i
                products = product_tile(q, slots, spans)
                if started:
                    products = products + lifted[q, :, cols]
                norm = jnp.concatenate([half_squares[q]] * len(slots), axis=1)
                scores = scale * (products - norm) + bias[:, 0:wide]
                lifted[q, :, cols] = scores
                high = jnp.maximum(high, jnp.max(scores.reshape(QROWS // 8, 8, wide), axis=0))
            return high

        high = lax.fori_loop(0, QUARTERS // STACK, score_tile, jnp.full((8, wide), -3e38, f32))
        high = jnp.max(high, axis=0, keepdims=True)

        def lift_tile(q, total):
            values = jnp.exp(lifted[q, :, cols] - high)
            lifted[q, :, cols] = values
            return total + jnp.sum(values.reshape(QROWS // 8, 8, wide), axis=0)

        total = lax.fori_loop(0, QUARTERS, lift_tile, jnp.zeros((8, wide), f32))
        total = jnp.sum(total, axis=0, keepdims=True)
        for k, slot in enumerate(slots):
            here = row_ids == where_from[slot]
            span = slice(k * LANES, (k + 1) * LANES)
            state["high"] = jnp.where(here, high[:, span], state["high"])
            state["total"] = jnp.where(here, total[:, span], state["total"])

    def turn(slot):
        span = pl.ds(slot * LANES, LANES)

        def tile(zz, carry):
            rows = pl.ds(pl.multiple_of(zz * PER, PER), PER)
            block = jnp.concatenate([lifted[q, rows, span] for q in (0, 2, 1, 3)], axis=0)
            turned[slot, :, pl.ds(pl.multiple_of(zz * LANES, LANES), LANES)] = block.T
            return carry

        lax.fori_loop(0, Z_CHIPS, tile, 0)

    for i in range(half):
        arrived(2, i)
        send_piece(2, i, right, 4)
        arrived(3, half + i)
        send_piece(3, half + i, left, 4)
        if i == 1:
            score((0,))
    for i in range(half):
        arrived(1, i)
        send_piece(1, i, right, 6)
        arrived(1, half + i)
        send_piece(1, half + i, left, 7)
        arrived(2, half + i)
        send_piece(2, half + i, y_peer, 6)
        arrived(3, i)
        send_piece(3, i, y_peer, 7)
        if i == 0:
            turn(0)
    score((1, 2))
    turn(1)
    turn(2)
    for i in range(half):
        arrived(4, i)
        arrived(4, half + i)
    for i in (3, 6, 7):
        send_piece(4, i, y_peer, 5)
    for i in range(2):
        arrived(6, half + i)
        send_piece(6, half + i, right, 5)
        arrived(7, i)
        send_piece(7, i, left, 5)
    score((3, 4))
    arrived(6, half + 2)
    arrived(7, 2)
    send_piece(7, 2, left, 5)
    turn(3)
    turn(4)
    arrived(6, PIECES - 1)
    arrived(7, half - 1)
    for i in range(half):
        arrived(6, i)
        arrived(7, half + i)
    score((6, 7))
    for i in (4, 0, 5, 1, 3):
        arrived(5, i)
    partial_score((5,), ((0, 2), (3, 6)))
    for i in (6, 2, 7):
        arrived(5, i)
    score((5,), ((2, 3), (6, 8)), True)

    my_high, my_total = state["high"], state["total"]
    stat_out[0:GROUP, :] = my_high
    stat_out[GROUP:2 * GROUP, :] = my_total
    stat_copies = []
    for r in range(1, GROUP):
        copy = pltpu.make_async_remote_copy(
            src_ref=stat_out, dst_ref=stat_in.at[STAT_SLOT[r]], send_sem=stat_send.at[r],
            recv_sem=stat_recv.at[STAT_SLOT[r]], device_id=peers[r], device_id_type=MESH)
        copy.start()
        sends.append(copy)
        stat_copies.append(copy)
    for slot in (6, 7, 5):
        turn(slot)
    for copy in stat_copies:
        copy.wait_recv()
    highest = my_high
    for r in range(1, GROUP):
        highest = jnp.maximum(highest, stat_in[r, 0:GROUP, :])
    my_part = jnp.exp(my_high - highest)
    whole = my_total * my_part
    for r in range(1, GROUP):
        whole = whole + stat_in[r, GROUP:2 * GROUP, :] * jnp.exp(stat_in[r, 0:GROUP, :] - highest)
    factor = my_part / whole
    factor_rows = [jnp.sum(jnp.where(row_ids == w, factor, 0.0), axis=0, keepdims=True) for w in where_from]
    factor_row = jnp.concatenate(factor_rows, axis=1)

    def weight_tile(q, carry):
        weights[q] = (lifted[q] * factor_row).astype(bf16)
        return carry

    lax.fori_loop(0, QUARTERS, weight_tile, 0)

    post_copies = []

    def give_posteriors(slot):
        columns = jnp.broadcast_to(factor_rows[slot], (LANES, LANES)).T
        for t in range(QUARTERS * QROWS // LANES):
            span = pl.ds(t * LANES, LANES)
            given[slot, :, span] = (turned[slot, :, span] * columns).astype(bf16)
        first = pl.multiple_of(where_from[slot] * ROWS, ROWS)
        copy = pltpu.make_async_copy(given.at[slot], posteriors.at[pl.ds(first, ROWS), :], post_sem.at[slot])
        copy.start()
        post_copies.append(copy)

    per_chunk = [chunk_refs[i * 7:(i + 1) * 7] for i in range(len(CHUNKS))]
    ring_copies = {}
    core_copies, y_copies = {}, {}
    mine_y = core * Y_HIGH

    def product(chunk, q):
        start, wide, counted, _ = chunk
        block = weights[q]
        rows = xbuf[:, :, pl.ds(start, wide)].reshape(GROUP * ROWS, wide)
        value = jnp.dot(block, rows, preferred_element_type=f32)
        if counted:
            ones = jnp.ones((GROUP * ROWS, LANES), bf16)
            value = jnp.concatenate([value, jnp.dot(block, ones, preferred_element_type=f32)], axis=1)
        return value

    def stage_core(j):
        to_core = per_chunk[j][0]
        for yy in range(Y_HIGH):
            to_core[yy] = product(CHUNKS[j], (1 - core) * Y_HIGH + yy).astype(bf16)
        copy = pltpu.make_async_remote_copy(
            src_ref=to_core, dst_ref=per_chunk[j][1], send_sem=core_send.at[j], recv_sem=core_recv.at[j],
            device_id=other_core, device_id_type=MESH)
        copy.start()
        sends.append(copy)
        core_copies[j] = copy

    def ring_start(j, step, up, src, dst):
        d = 0 if up else 1
        copy = pltpu.make_async_remote_copy(
            src_ref=src, dst_ref=dst, send_sem=ring_send.at[j, step, d], recv_sem=ring_recv.at[j, step, d],
            device_id=z_up if up else z_down, device_id_type=MESH)
        copy.start()
        sends.append(copy)
        ring_copies[(j, step, d)] = copy

    def ring_first(j):
        out, into = per_chunk[j][3], per_chunk[j][4]
        rows = out.shape[2]
        mid = rows // 2
        values = local_rows(j, 4).astype(bf16)
        out[0, 0, 0:mid] = values[0:mid]
        out[0, 1, 0:mid] = values[mid:rows]
        for d in range(2):
            ring_start(j, 0, d == 0, out.at[0, d, pl.ds(0, mid)], into.at[0, d, pl.ds(0, mid)])

    def ring_next(j, step):
        out, into = per_chunk[j][3], per_chunk[j][4]
        rows = out.shape[2]
        mid = rows // 2
        for d in range(2):
            mine = local_rows(j, 4 - step if d == 0 else 4 + step)
            ring_copies[(j, step - 1, d)].wait_recv()
            if step == 1:
                got = into[0, d, 0:mid].astype(f32)
                if d == 0:
                    out[1, d, 0:mid] = (mine[0:mid] + got).astype(bf16)
                    out[1, d, mid:rows] = mine[mid:rows].astype(bf16)
                else:
                    out[1, d, 0:mid] = mine[0:mid].astype(bf16)
                    out[1, d, mid:rows] = (mine[mid:rows] + got).astype(bf16)
            else:
                out[step, d] = (mine + into[step - 1, d].astype(f32)).astype(bf16)
            ring_start(j, step, d == 0, out.at[step, d], into.at[step, d])

    def ring_sum(j):
        into = per_chunk[j][4]
        mine = local_rows(j, 0)
        for d in range(2):
            ring_copies[(j, 3, d)].wait_recv()
        return mine + into[3, 0].astype(f32) + into[3, 1].astype(f32)

    def y_start(j):
        copy = pltpu.make_async_remote_copy(
            src_ref=per_chunk[j][5], dst_ref=per_chunk[j][6], send_sem=y_send.at[j, 0], recv_sem=y_recv.at[j, 0],
            device_id=y_far, device_id_type=MESH)
        copy.start()
        sends.append(copy)
        y_copies[j] = copy

    def y_slices(j, steps):
        for step in steps:
            which = (z + step) % Z_CHIPS
            copy = pltpu.make_async_remote_copy(
                src_ref=per_chunk[j][5].at[which], dst_ref=per_chunk[j][6].at[which], send_sem=y_send.at[j, step],
                recv_sem=y_recv.at[j, step], device_id=y_far, device_id_type=MESH)
            copy.start()
            sends.append(copy)
            y_copies[(j, step)] = copy

    def local_rows(j, step):
        which = (z + step) % Z_CHIPS
        if CHUNKS[j][3] == "z":
            return per_chunk[j][2][which]
        y_copies[(j, step)].wait_recv()
        return per_chunk[j][2][which] + per_chunk[j][6][which].astype(f32)

    def stage_local(j):
        from_core, local = per_chunk[j][1], per_chunk[j][2]
        wide = width_of(CHUNKS[j])
        z_first = CHUNKS[j][3] == "z"

        def own(yy):
            value = product(CHUNKS[j], mine_y + yy) + from_core[yy].astype(f32)
            return value.reshape(Z_CHIPS, PER, wide)

        core_copies[j].wait_recv()
        if z_first:
            for yy in range(Y_HIGH):
                local[:, pl.ds(yy * PER, PER), :] = own(yy)
            ring_first(j)
        else:
            per_chunk[j][5][...] = own(1 - y_hi).astype(bf16)
            local[...] = own(y_hi)
            y_slices(j, (4, 3, 5))

    state["divide"] = None
    waiting = []

    def finish(j, value):
        start, wide, counted, _ = CHUNKS[j]
        if counted:
            state["divide"] = value[:, wide:wide + LANES] + prior_weight
        prior = table[mine_y + y_hi, z, :, pl.ds(start, wide)].astype(f32)
        references[:, pl.ds(start, wide)] = value[:, 0:wide] + prior_weight * prior
        waiting.append((start, wide))
        if state["divide"] is not None:
            for first, columns in waiting:
                below = jnp.concatenate([state["divide"]] * (columns // LANES), axis=1)
                references[:, pl.ds(first, columns)] = references[:, pl.ds(first, columns)] / below
            waiting.clear()

    def stages(j):
        if CHUNKS[j][3] == "z":
            def to_y():
                local = per_chunk[j][2]
                local[z] = ring_sum(j)
                per_chunk[j][5][...] = local[z, pl.ds(pl.multiple_of((1 - y_hi) * PER, PER), PER), :].astype(bf16)
                y_start(j)

            def last():
                y_copies[j].wait_recv()
                mine = per_chunk[j][2][z, pl.ds(pl.multiple_of(y_hi * PER, PER), PER), :]
                finish(j, mine + per_chunk[j][6][...].astype(f32))

            return [lambda: stage_core(j), lambda: stage_local(j), lambda: ring_next(j, 1), lambda: ring_next(j, 2),
                    lambda: ring_next(j, 3), to_y, last]

        return [lambda: stage_core(j), lambda: stage_local(j), lambda: y_slices(j, (2, 6, 1, 7, 0)), lambda: ring_first(j),
                lambda: ring_next(j, 1), lambda: ring_next(j, 2), lambda: ring_next(j, 3), lambda: finish(j, ring_sum(j))]

    pl.semaphore_wait(ready, 2)
    plans = [stages(j) for j in range(len(CHUNKS))]
    for place, (j, s) in enumerate(ORDER):
        plans[j][s]()
        if place % 4 == 3 and place // 4 < GROUP:
            give_posteriors(place // 4)

    for copy in sends:
        copy.wait_send()
    for copy in post_copies:
        copy.wait()


def scratch():
    shapes = [
        pltpu.VMEM((GROUP, ROWS), f32),
        pltpu.SMEM((GROUP, Z_CHIPS), jnp.int32),
        pltpu.VMEM((ROWS, DEPTH), f32),
        pltpu.VMEM((GROUP, ROWS, DEPTH), bf16),
        pltpu.VMEM((QUARTERS, Z_CHIPS, PER, DEPTH), bf16),
        pltpu.VMEM((QUARTERS, QROWS, LANES), f32),
        pltpu.VMEM((QROWS, 2 * LANES), f32),
        pltpu.VMEM((QUARTERS, QROWS, GROUP * ROWS), f32),
        pltpu.VMEM((QUARTERS, QROWS, GROUP * ROWS), bf16),
        pltpu.VMEM((GROUP, ROWS, QUARTERS * QROWS), f32),
        pltpu.VMEM((GROUP, ROWS, QUARTERS * QROWS), bf16),
        pltpu.VMEM((2 * GROUP, LANES), f32),
        pltpu.VMEM((GROUP, 2 * GROUP, LANES), f32),
        pltpu.SemaphoreType.REGULAR,
        pltpu.SemaphoreType.DMA((PIECES + 2 + QUARTERS,)),
        pltpu.SemaphoreType.DMA((7 * PIECES,)),
        pltpu.SemaphoreType.DMA((GROUP, PIECES)),
        pltpu.SemaphoreType.DMA((GROUP,)),
        pltpu.SemaphoreType.DMA((GROUP,)),
        pltpu.SemaphoreType.DMA((GROUP,)),
        pltpu.SemaphoreType.DMA((len(CHUNKS),)),
        pltpu.SemaphoreType.DMA((len(CHUNKS),)),
        pltpu.SemaphoreType.DMA((len(CHUNKS), 4, 2)),
        pltpu.SemaphoreType.DMA((len(CHUNKS), 4, 2)),
        pltpu.SemaphoreType.DMA((len(CHUNKS), Z_CHIPS)),
        pltpu.SemaphoreType.DMA((len(CHUNKS), Z_CHIPS)),
    ]
    for chunk in CHUNKS:
        wide = width_of(chunk)
        z_first = chunk[3] == "z"
        rows = Y_HIGH * PER if z_first else PER
        y_shape = (PER, wide) if z_first else (Z_CHIPS, PER, wide)
        shapes += [
            pltpu.VMEM((Y_HIGH, QROWS, wide), bf16),
            pltpu.VMEM((Y_HIGH, QROWS, wide), bf16),
            pltpu.VMEM((Z_CHIPS, rows, wide), f32),
            pltpu.VMEM((4, 2, rows, wide), bf16),
            pltpu.VMEM((4, 2, rows, wide), bf16),
            pltpu.VMEM(y_shape, bf16),
            pltpu.VMEM(y_shape, bf16),
        ]
    return shapes


def hand_over(posts, refs, posts_out, refs_out, sem):
    rows = GROUP * ROWS // HANDS
    spans = [pl.ds(i * rows, rows) for i in range(HANDS)]
    copies = [pltpu.make_async_copy(posts.at[s], posts_out.at[s], sem.at[i]) for i, s in enumerate(spans)]
    copies.append(pltpu.make_async_copy(refs, refs_out, sem.at[HANDS]))
    for copy in copies:
        copy.start()
    for copy in copies:
        copy.wait()


def body(images, precision, projections, tile_mask):
    posts, refs = pl.pallas_call(
        kernel,
        out_shape=(
            jax.ShapeDtypeStruct((GROUP * ROWS, QUARTERS * QROWS), bf16),
            jax.ShapeDtypeStruct((PER, DEPTH), f32),
        ),
        in_specs=[
            pl.BlockSpec(memory_space=pltpu.HBM),
            pl.BlockSpec(memory_space=pltpu.HBM),
            pl.BlockSpec(memory_space=pltpu.HBM),
            pl.BlockSpec(memory_space=pltpu.HBM),
        ],
        out_specs=(pl.BlockSpec(memory_space=pl.ANY), pl.BlockSpec(memory_space=pltpu.VMEM)),
        scratch_shapes=scratch(),
        compiler_params=pltpu.CompilerParams(
            collective_id=0, has_side_effects=True, vmem_limit_bytes=40 * 1024 * 1024
        ),
    )(*[pltpu.with_memory_space_constraint(v, pltpu.HBM) for v in (images, precision.reshape(GROUP, ROWS), projections.reshape(Z_CHIPS, Y_HIGH, CORES, PER, DEPTH), tile_mask)])
    return pl.pallas_call(
        hand_over,
        out_shape=(jax.ShapeDtypeStruct(posts.shape, bf16), jax.ShapeDtypeStruct(refs.shape, f32)),
        in_specs=[pl.BlockSpec(memory_space=pl.ANY)] * 2,
        out_specs=(pl.BlockSpec(memory_space=pltpu.HBM), pl.BlockSpec(memory_space=pltpu.HBM)),
        scratch_shapes=[pltpu.SemaphoreType.DMA((HANDS + 1,))],
        compiler_params=pltpu.CompilerParams(vmem_limit_bytes=4 * 1024 * 1024),
    )(posts, refs)


def solution(mesh):
    return jax.shard_map(
        body,
        mesh=mesh,
        in_specs=(P(("img", "ori"), None), P("img"), P("ori", None), P("img", "ori")),
        out_specs=(P("img", "ori"), P(("ori", "img"), None)),
        check_vma=False,
    )
```

```python
import jax
import jax.numpy as jnp
from jax import lax
from jax.experimental import pallas as pl
from jax.experimental.pallas import tpu as pltpu
from jax.sharding import PartitionSpec as P

MESH = pl.DeviceIdType.MESH
prior_weight = 1.0
very_low = -1e30

X_CHIPS, Y_LOW = 4, 2
Z_CHIPS, Y_HIGH, CORES = 8, 2, 2
GROUP = X_CHIPS * Y_LOW
HANDS = 2
ROWS = 128
DEPTH = 2048
PER = 32
QUARTERS = CORES * Y_HIGH
QROWS = Z_CHIPS * PER
LANES = 128
PIECES = 8
STACK = 2
PIECE = DEPTH // PIECES
PIECE_ORDER = (0, 4, 1, 5, 2, 6, 3, 7)
CHUNKS = (
    (0, 256, False, "z"),
    (256, 256, False, "z"),
    (512, 256, False, "y"),
    (768, 256, True, "y"),
    (1024, 256, False, "z"),
    (1280, 256, False, "y"),
    (1536, 256, False, "z"),
    (1792, 256, False, "y"),
)
ORDER = (
    (0, 0), (1, 0), (2, 0), (3, 0), (4, 0), (5, 0), (6, 0), (0, 1), (1, 1), (2, 1), (7, 0), (3, 1),
    (4, 1), (5, 1), (0, 2), (6, 1), (1, 2), (7, 1), (7, 2), (3, 2), (5, 2), (2, 2), (2, 3), (4, 2),
    (3, 3), (0, 3), (6, 2), (1, 3), (5, 3), (2, 4), (7, 3), (4, 3), (3, 4), (0, 4), (6, 3), (1, 4),
    (5, 4), (7, 4), (4, 4), (3, 5), (0, 5), (6, 4), (1, 5), (5, 5), (7, 5), (2, 5), (4, 5), (3, 6),
    (0, 6), (6, 5), (5, 6), (7, 6), (1, 6), (2, 6), (3, 7), (4, 6), (5, 7), (6, 6), (7, 7), (2, 7),
)
STAT_SLOT = {1: 1, 2: 3, 3: 2, 4: 4, 5: 5, 6: 7, 7: 6}

f32 = jnp.float32
bf16 = jnp.bfloat16


def width_of(chunk):
    return chunk[1] + (LANES if chunk[2] else 0)


def kernel(images, precision_hbm, projections, mask_hbm, posteriors, references, precision, tile_mask, raw, xbuf, table, half_squares, bias, lifted,
           weights, turned, given, stat_out, stat_in, ready, load_sem, piece_send, piece_recv, stat_send, stat_recv, post_sem,
           core_send, core_recv, ring_send, ring_recv, y_send, y_recv, *chunk_refs):
    img, ori = lax.axis_index("img"), lax.axis_index("ori")
    z, y_hi, core = img // 4, (img // 2) % 2, img % 2
    x, y_lo = ori // 2, ori % 2

    def at_ori(dx, flip):
        row = 1 - y_lo if flip else y_lo
        return ((x + dx) % X_CHIPS) * 2 + row

    where_from = [at_ori(0, False), at_ori(0, True), at_ori(3, False), at_ori(1, False),
                  at_ori(2, False), at_ori(2, True), at_ori(3, True), at_ori(1, True)]
    peers = [(img, w) for w in where_from]
    y_peer, left, right = peers[1], peers[2], peers[3]
    other_core = (z * 4 + y_hi * 2 + 1 - core, ori)
    z_up = (((z + 1) % Z_CHIPS) * 4 + y_hi * 2 + core, ori)
    z_down = (((z + 7) % Z_CHIPS) * 4 + y_hi * 2 + core, ori)
    y_far = (z * 4 + (1 - y_hi) * 2 + core, ori)

    load_images = []
    for i in PIECE_ORDER:
        span = pl.ds(i * PIECE, PIECE)
        load_images.append(pltpu.make_async_copy(images.at[:, span], raw.at[:, span], load_sem.at[i]))
        load_images[-1].start()
    load_small = [pltpu.make_async_copy(precision_hbm, precision, load_sem.at[PIECES]),
                  pltpu.make_async_copy(mask_hbm, tile_mask, load_sem.at[PIECES + 1])]
    load_table = []
    for c in range(CORES):
        for yy in range(Y_HIGH):
            q = c * Y_HIGH + yy
            load_table.append(
                pltpu.make_async_copy(projections.at[:, yy, c], table.at[q], load_sem.at[PIECES + 2 + q]))

    barrier = pltpu.get_barrier_semaphore()
    y = y_hi * Y_LOW + y_lo
    y_sides = []
    for step in (1, 3):
        there = (y + step) % (Y_HIGH * Y_LOW)
        y_sides.append((z * 4 + (there // Y_LOW) * 2 + core, x * 2 + there % Y_LOW))
    friends = y_sides + [left, right, other_core, z_up, z_down]
    for friend in friends:
        pl.semaphore_signal(barrier, inc=1, device_id=friend, device_id_type=MESH)

    def lower(place):
        load_images[place].wait()
        span = pl.ds(PIECE_ORDER[place] * PIECE, PIECE)
        xbuf[0, :, span] = raw[:, span].astype(bf16)

    for place in range(2):
        lower(place)
    pl.semaphore_wait(barrier, len(friends))
    for side in y_sides:
        pl.semaphore_signal(ready, inc=1, device_id=side, device_id_type=MESH)

    sends = []
    arrivals = {}
    counter = [0]

    def send_piece(slot, piece, target, far_slot):
        span = pl.ds(piece * PIECE, PIECE)
        copy = pltpu.make_async_remote_copy(
            src_ref=xbuf.at[slot, :, span], dst_ref=xbuf.at[far_slot, :, span], send_sem=piece_send.at[counter[0]],
            recv_sem=piece_recv.at[far_slot, piece], device_id=target, device_id_type=MESH)
        counter[0] += 1
        copy.start()
        sends.append(copy)
        arrivals[(far_slot, piece)] = copy

    def arrived(slot, piece):
        arrivals[(slot, piece)].wait_recv()

    half = PIECES // 2
    for i in range(half):
        if i > 0:
            lower(2 * i)
            lower(2 * i + 1)
        send_piece(0, i, right, 2)
        send_piece(0, half + i, left, 3)
        send_piece(0, i, y_peer, 1)
        send_piece(0, half + i, y_peer, 1)
    for i in range(half):
        send_piece(0, half + i, right, 2)
        send_piece(0, i, left, 3)

    for copy in load_small + load_table:
        copy.start()
    for copy in load_small + load_table:
        copy.wait()

    def square_tile(q, carry):
        wide = table[q].reshape(QROWS, DEPTH).astype(f32)
        total = jnp.sum(wide * wide, axis=1, keepdims=True)
        half_squares[q] = jnp.broadcast_to(0.5 * total, (QROWS, LANES))
        return carry

    lax.fori_loop(0, QUARTERS, square_tile, 0)

    row_ids = lax.broadcasted_iota(jnp.int32, (GROUP, LANES), 0)
    state = {"high": jnp.zeros((GROUP, LANES), f32), "total": jnp.zeros((GROUP, LANES), f32)}

    def product_tile(q, slots, spans):
        total = None
        for first, last in spans:
            span = pl.ds(first * PIECE, (last - first) * PIECE)
            block = table[q, :, :, span].reshape(QROWS, (last - first) * PIECE)
            rows = xbuf[pl.ds(slots[0], len(slots)), :, span].reshape(len(slots) * ROWS, (last - first) * PIECE)
            part = lax.dot_general(block, rows, (((1,), (1,)), ((), ())), preferred_element_type=f32)
            total = part if total is None else total + part
        return total

    def partial_score(slots, spans):
        cols = pl.ds(slots[0] * LANES, len(slots) * LANES)

        def tile(t, carry):
            for i in range(STACK):
                q = t * STACK + i
                lifted[q, :, cols] = product_tile(q, slots, spans)
            return carry

        lax.fori_loop(0, QUARTERS // STACK, tile, 0)

    def score(slots, spans=((0, PIECES),), started=False):
        wide = len(slots) * LANES
        cols = pl.ds(slots[0] * LANES, wide)
        for k, slot in enumerate(slots):
            for zz in range(Z_CHIPS):
                live = jnp.where(tile_mask[where_from[slot], zz] > 0, 0.0, very_low)
                bias[pl.ds(zz * PER, PER), pl.ds(k * LANES, LANES)] = jnp.full((PER, LANES), live, f32)
        scale = jnp.concatenate([precision[pl.ds(where_from[slot], 1), :] for slot in slots], axis=1)

        def score_tile(t, high):
            for i in range(STACK):
                q = t * STACK + i
                products = product_tile(q, slots, spans)
                if started:
                    products = products + lifted[q, :, cols]
                norm = jnp.concatenate([half_squares[q]] * len(slots), axis=1)
                scores = scale * (products - norm) + bias[:, 0:wide]
                lifted[q, :, cols] = scores
                high = jnp.maximum(high, jnp.max(scores.reshape(QROWS // 8, 8, wide), axis=0))
            return high

        high = lax.fori_loop(0, QUARTERS // STACK, score_tile, jnp.full((8, wide), -3e38, f32))
        high = jnp.max(high, axis=0, keepdims=True)

        def lift_tile(q, total):
            values = jnp.exp(lifted[q, :, cols] - high)
            lifted[q, :, cols] = values
            return total + jnp.sum(values.reshape(QROWS // 8, 8, wide), axis=0)

        total = lax.fori_loop(0, QUARTERS, lift_tile, jnp.zeros((8, wide), f32))
        total = jnp.sum(total, axis=0, keepdims=True)
        for k, slot in enumerate(slots):
            here = row_ids == where_from[slot]
            span = slice(k * LANES, (k + 1) * LANES)
            state["high"] = jnp.where(here, high[:, span], state["high"])
            state["total"] = jnp.where(here, total[:, span], state["total"])

    def turn(slot):
        span = pl.ds(slot * LANES, LANES)

        def tile(zz, carry):
            rows = pl.ds(pl.multiple_of(zz * PER, PER), PER)
            block = jnp.concatenate([lifted[q, rows, span] for q in (0, 2, 1, 3)], axis=0)
            turned[slot, :, pl.ds(pl.multiple_of(zz * LANES, LANES), LANES)] = block.T
            return carry

        lax.fori_loop(0, Z_CHIPS, tile, 0)

    for i in range(half):
        arrived(2, i)
        send_piece(2, i, right, 4)
        arrived(3, half + i)
        send_piece(3, half + i, left, 4)
        if i == 1:
            score((0,))
    for i in range(half):
        arrived(1, i)
        send_piece(1, i, right, 6)
        arrived(1, half + i)
        send_piece(1, half + i, left, 7)
        arrived(2, half + i)
        send_piece(2, half + i, y_peer, 6)
        arrived(3, i)
        send_piece(3, i, y_peer, 7)
        if i == 0:
            turn(0)
    score((1, 2))
    turn(1)
    turn(2)
    for i in range(half):
        arrived(4, i)
        arrived(4, half + i)
    for i in (3, 6, 7):
        send_piece(4, i, y_peer, 5)
    for i in range(2):
        arrived(6, half + i)
        send_piece(6, half + i, right, 5)
        arrived(7, i)
        send_piece(7, i, left, 5)
    score((3, 4))
    arrived(6, half + 2)
    arrived(7, 2)
    send_piece(7, 2, left, 5)
    turn(3)
    turn(4)
    arrived(6, PIECES - 1)
    arrived(7, half - 1)
    for i in range(half):
        arrived(6, i)
        arrived(7, half + i)
    score((6, 7))
    for i in (4, 0, 5, 1, 3, 6):
        arrived(5, i)
    partial_score((5,), ((0, 2), (3, 7)))
    for i in (2, 7):
        arrived(5, i)
    score((5,), ((2, 3), (7, 8)), True)

    my_high, my_total = state["high"], state["total"]
    stat_out[0:GROUP, :] = my_high
    stat_out[GROUP:2 * GROUP, :] = my_total
    stat_copies = []
    for r in range(1, GROUP):
        copy = pltpu.make_async_remote_copy(
            src_ref=stat_out, dst_ref=stat_in.at[STAT_SLOT[r]], send_sem=stat_send.at[r],
            recv_sem=stat_recv.at[STAT_SLOT[r]], device_id=peers[r], device_id_type=MESH)
        copy.start()
        sends.append(copy)
        stat_copies.append(copy)
    for slot in (6, 7, 5):
        turn(slot)
    for copy in stat_copies:
        copy.wait_recv()
    highest = my_high
    for r in range(1, GROUP):
        highest = jnp.maximum(highest, stat_in[r, 0:GROUP, :])
    my_part = jnp.exp(my_high - highest)
    whole = my_total * my_part
    for r in range(1, GROUP):
        whole = whole + stat_in[r, GROUP:2 * GROUP, :] * jnp.exp(stat_in[r, 0:GROUP, :] - highest)
    factor = my_part / whole
    factor_rows = [jnp.sum(jnp.where(row_ids == w, factor, 0.0), axis=0, keepdims=True) for w in where_from]
    factor_row = jnp.concatenate(factor_rows, axis=1)

    def weight_tile(q, carry):
        weights[q] = (lifted[q] * factor_row).astype(bf16)
        return carry

    lax.fori_loop((1 - core) * Y_HIGH, (1 - core) * Y_HIGH + Y_HIGH, weight_tile, 0)

    post_copies = []

    def give_posteriors(slot):
        columns = jnp.broadcast_to(factor_rows[slot], (LANES, LANES)).T
        for t in range(QUARTERS * QROWS // LANES):
            span = pl.ds(t * LANES, LANES)
            given[slot, :, span] = (turned[slot, :, span] * columns).astype(bf16)
        first = pl.multiple_of(where_from[slot] * ROWS, ROWS)
        copy = pltpu.make_async_copy(given.at[slot], posteriors.at[pl.ds(first, ROWS), :], post_sem.at[slot])
        copy.start()
        post_copies.append(copy)

    per_chunk = [chunk_refs[i * 7:(i + 1) * 7] for i in range(len(CHUNKS))]
    ring_copies = {}
    core_copies, y_copies = {}, {}
    mine_y = core * Y_HIGH

    def product(chunk, q):
        start, wide, counted, _ = chunk
        block = weights[q]
        rows = xbuf[:, :, pl.ds(start, wide)].reshape(GROUP * ROWS, wide)
        value = jnp.dot(block, rows, preferred_element_type=f32)
        if counted:
            ones = jnp.ones((GROUP * ROWS, LANES), bf16)
            value = jnp.concatenate([value, jnp.dot(block, ones, preferred_element_type=f32)], axis=1)
        return value

    def stage_core(j):
        to_core = per_chunk[j][0]
        for yy in range(Y_HIGH):
            to_core[yy] = product(CHUNKS[j], (1 - core) * Y_HIGH + yy).astype(bf16)
        copy = pltpu.make_async_remote_copy(
            src_ref=to_core, dst_ref=per_chunk[j][1], send_sem=core_send.at[j], recv_sem=core_recv.at[j],
            device_id=other_core, device_id_type=MESH)
        copy.start()
        sends.append(copy)
        core_copies[j] = copy

    def ring_start(j, step, up, src, dst):
        d = 0 if up else 1
        copy = pltpu.make_async_remote_copy(
            src_ref=src, dst_ref=dst, send_sem=ring_send.at[j, step, d], recv_sem=ring_recv.at[j, step, d],
            device_id=z_up if up else z_down, device_id_type=MESH)
        copy.start()
        sends.append(copy)
        ring_copies[(j, step, d)] = copy

    def ring_first(j):
        out, into = per_chunk[j][3], per_chunk[j][4]
        rows = out.shape[2]
        mid = rows // 2
        values = local_rows(j, 4).astype(bf16)
        out[0, 0, 0:mid] = values[0:mid]
        out[0, 1, 0:mid] = values[mid:rows]
        for d in range(2):
            ring_start(j, 0, d == 0, out.at[0, d, pl.ds(0, mid)], into.at[0, d, pl.ds(0, mid)])

    def ring_next(j, step):
        out, into = per_chunk[j][3], per_chunk[j][4]
        rows = out.shape[2]
        mid = rows // 2
        for d in range(2):
            mine = local_rows(j, 4 - step if d == 0 else 4 + step)
            ring_copies[(j, step - 1, d)].wait_recv()
            if step == 1:
                got = into[0, d, 0:mid].astype(f32)
                if d == 0:
                    out[1, d, 0:mid] = (mine[0:mid] + got).astype(bf16)
                    out[1, d, mid:rows] = mine[mid:rows].astype(bf16)
                else:
                    out[1, d, 0:mid] = mine[0:mid].astype(bf16)
                    out[1, d, mid:rows] = (mine[mid:rows] + got).astype(bf16)
            else:
                out[step, d] = (mine + into[step - 1, d].astype(f32)).astype(bf16)
            ring_start(j, step, d == 0, out.at[step, d], into.at[step, d])

    def ring_sum(j):
        into = per_chunk[j][4]
        mine = local_rows(j, 0)
        for d in range(2):
            ring_copies[(j, 3, d)].wait_recv()
        return mine + into[3, 0].astype(f32) + into[3, 1].astype(f32)

    def y_start(j):
        copy = pltpu.make_async_remote_copy(
            src_ref=per_chunk[j][5], dst_ref=per_chunk[j][6], send_sem=y_send.at[j, 0], recv_sem=y_recv.at[j, 0],
            device_id=y_far, device_id_type=MESH)
        copy.start()
        sends.append(copy)
        y_copies[j] = copy

    def y_slices(j, steps):
        for step in steps:
            which = (z + step) % Z_CHIPS
            copy = pltpu.make_async_remote_copy(
                src_ref=per_chunk[j][5].at[which], dst_ref=per_chunk[j][6].at[which], send_sem=y_send.at[j, step],
                recv_sem=y_recv.at[j, step], device_id=y_far, device_id_type=MESH)
            copy.start()
            sends.append(copy)
            y_copies[(j, step)] = copy

    def local_rows(j, step):
        which = (z + step) % Z_CHIPS
        if CHUNKS[j][3] == "z":
            return per_chunk[j][2][which]
        y_copies[(j, step)].wait_recv()
        return per_chunk[j][2][which] + per_chunk[j][6][which].astype(f32)

    def stage_local(j):
        from_core, local = per_chunk[j][1], per_chunk[j][2]
        wide = width_of(CHUNKS[j])
        z_first = CHUNKS[j][3] == "z"

        def own(yy):
            value = product(CHUNKS[j], mine_y + yy) + from_core[yy].astype(f32)
            return value.reshape(Z_CHIPS, PER, wide)

        core_copies[j].wait_recv()
        if z_first:
            for yy in range(Y_HIGH):
                local[:, pl.ds(yy * PER, PER), :] = own(yy)
            ring_first(j)
        else:
            per_chunk[j][5][...] = own(1 - y_hi).astype(bf16)
            local[...] = own(y_hi)
            y_slices(j, (4, 3, 5))

    state["divide"] = None
    waiting = []

    def finish(j, value):
        start, wide, counted, _ = CHUNKS[j]
        if counted:
            state["divide"] = value[:, wide:wide + LANES] + prior_weight
        prior = table[mine_y + y_hi, z, :, pl.ds(start, wide)].astype(f32)
        references[:, pl.ds(start, wide)] = value[:, 0:wide] + prior_weight * prior
        waiting.append((start, wide))
        if state["divide"] is not None:
            for first, columns in waiting:
                below = jnp.concatenate([state["divide"]] * (columns // LANES), axis=1)
                references[:, pl.ds(first, columns)] = references[:, pl.ds(first, columns)] / below
            waiting.clear()

    def stages(j):
        if CHUNKS[j][3] == "z":
            def to_y():
                local = per_chunk[j][2]
                local[z] = ring_sum(j)
                per_chunk[j][5][...] = local[z, pl.ds(pl.multiple_of((1 - y_hi) * PER, PER), PER), :].astype(bf16)
                y_start(j)

            def last():
                y_copies[j].wait_recv()
                mine = per_chunk[j][2][z, pl.ds(pl.multiple_of(y_hi * PER, PER), PER), :]
                finish(j, mine + per_chunk[j][6][...].astype(f32))

            return [lambda: stage_core(j), lambda: stage_local(j), lambda: ring_next(j, 1), lambda: ring_next(j, 2),
                    lambda: ring_next(j, 3), to_y, last]

        return [lambda: stage_core(j), lambda: stage_local(j), lambda: y_slices(j, (2, 6, 1, 7, 0)), lambda: ring_first(j),
                lambda: ring_next(j, 1), lambda: ring_next(j, 2), lambda: ring_next(j, 3), lambda: finish(j, ring_sum(j))]

    pl.semaphore_wait(ready, 2)
    plans = [stages(j) for j in range(len(CHUNKS))]
    for place, (j, s) in enumerate(ORDER):
        plans[j][s]()
        if place == 0:
            lax.fori_loop(core * Y_HIGH, core * Y_HIGH + Y_HIGH, weight_tile, 0)
        if place % 4 == 3 and place // 4 < GROUP:
            give_posteriors(place // 4)

    for copy in sends:
        copy.wait_send()
    for copy in post_copies:
        copy.wait()


def scratch():
    shapes = [
        pltpu.VMEM((GROUP, ROWS), f32),
        pltpu.SMEM((GROUP, Z_CHIPS), jnp.int32),
        pltpu.VMEM((ROWS, DEPTH), f32),
        pltpu.VMEM((GROUP, ROWS, DEPTH), bf16),
        pltpu.VMEM((QUARTERS, Z_CHIPS, PER, DEPTH), bf16),
        pltpu.VMEM((QUARTERS, QROWS, LANES), f32),
        pltpu.VMEM((QROWS, 2 * LANES), f32),
        pltpu.VMEM((QUARTERS, QROWS, GROUP * ROWS), f32),
        pltpu.VMEM((QUARTERS, QROWS, GROUP * ROWS), bf16),
        pltpu.VMEM((GROUP, ROWS, QUARTERS * QROWS), f32),
        pltpu.VMEM((GROUP, ROWS, QUARTERS * QROWS), bf16),
        pltpu.VMEM((2 * GROUP, LANES), f32),
        pltpu.VMEM((GROUP, 2 * GROUP, LANES), f32),
        pltpu.SemaphoreType.REGULAR,
        pltpu.SemaphoreType.DMA((PIECES + 2 + QUARTERS,)),
        pltpu.SemaphoreType.DMA((7 * PIECES,)),
        pltpu.SemaphoreType.DMA((GROUP, PIECES)),
        pltpu.SemaphoreType.DMA((GROUP,)),
        pltpu.SemaphoreType.DMA((GROUP,)),
        pltpu.SemaphoreType.DMA((GROUP,)),
        pltpu.SemaphoreType.DMA((len(CHUNKS),)),
        pltpu.SemaphoreType.DMA((len(CHUNKS),)),
        pltpu.SemaphoreType.DMA((len(CHUNKS), 4, 2)),
        pltpu.SemaphoreType.DMA((len(CHUNKS), 4, 2)),
        pltpu.SemaphoreType.DMA((len(CHUNKS), Z_CHIPS)),
        pltpu.SemaphoreType.DMA((len(CHUNKS), Z_CHIPS)),
    ]
    for chunk in CHUNKS:
        wide = width_of(chunk)
        z_first = chunk[3] == "z"
        rows = Y_HIGH * PER if z_first else PER
        y_shape = (PER, wide) if z_first else (Z_CHIPS, PER, wide)
        shapes += [
            pltpu.VMEM((Y_HIGH, QROWS, wide), bf16),
            pltpu.VMEM((Y_HIGH, QROWS, wide), bf16),
            pltpu.VMEM((Z_CHIPS, rows, wide), f32),
            pltpu.VMEM((4, 2, rows, wide), bf16),
            pltpu.VMEM((4, 2, rows, wide), bf16),
            pltpu.VMEM(y_shape, bf16),
            pltpu.VMEM(y_shape, bf16),
        ]
    return shapes


def hand_over(posts, refs, posts_out, refs_out, sem):
    rows = GROUP * ROWS // HANDS
    spans = [pl.ds(i * rows, rows) for i in range(HANDS)]
    copies = [pltpu.make_async_copy(posts.at[s], posts_out.at[s], sem.at[i]) for i, s in enumerate(spans)]
    copies.append(pltpu.make_async_copy(refs, refs_out, sem.at[HANDS]))
    for copy in copies:
        copy.start()
    for copy in copies:
        copy.wait()


def body(images, precision, projections, tile_mask):
    posts, refs = pl.pallas_call(
        kernel,
        out_shape=(
            jax.ShapeDtypeStruct((GROUP * ROWS, QUARTERS * QROWS), bf16),
            jax.ShapeDtypeStruct((PER, DEPTH), f32),
        ),
        in_specs=[
            pl.BlockSpec(memory_space=pltpu.HBM),
            pl.BlockSpec(memory_space=pltpu.HBM),
            pl.BlockSpec(memory_space=pltpu.HBM),
            pl.BlockSpec(memory_space=pltpu.HBM),
        ],
        out_specs=(pl.BlockSpec(memory_space=pl.ANY), pl.BlockSpec(memory_space=pltpu.VMEM)),
        scratch_shapes=scratch(),
        compiler_params=pltpu.CompilerParams(
            collective_id=0, has_side_effects=True, vmem_limit_bytes=40 * 1024 * 1024
        ),
    )(*[pltpu.with_memory_space_constraint(v, pltpu.HBM) for v in (images, precision.reshape(GROUP, ROWS), projections.reshape(Z_CHIPS, Y_HIGH, CORES, PER, DEPTH), tile_mask)])
    return pl.pallas_call(
        hand_over,
        out_shape=(jax.ShapeDtypeStruct(posts.shape, bf16), jax.ShapeDtypeStruct(refs.shape, f32)),
        in_specs=[pl.BlockSpec(memory_space=pl.ANY)] * 2,
        out_specs=(pl.BlockSpec(memory_space=pltpu.HBM), pl.BlockSpec(memory_space=pltpu.HBM)),
        scratch_shapes=[pltpu.SemaphoreType.DMA((HANDS + 1,))],
        compiler_params=pltpu.CompilerParams(vmem_limit_bytes=4 * 1024 * 1024),
    )(posts, refs)


def solution(mesh):
    return jax.shard_map(
        body,
        mesh=mesh,
        in_specs=(P(("img", "ori"), None), P("img"), P("ori", None), P("img", "ori")),
        out_specs=(P("img", "ori"), P(("ori", "img"), None)),
        check_vma=False,
    )
```

```python
import jax
import jax.numpy as jnp
from jax import lax
from jax.experimental import pallas as pl
from jax.experimental.pallas import tpu as pltpu
from jax.sharding import PartitionSpec as P

MESH = pl.DeviceIdType.MESH
prior_weight = 1.0
very_low = -1e30

X_CHIPS, Y_LOW = 4, 2
Z_CHIPS, Y_HIGH, CORES = 8, 2, 2
GROUP = X_CHIPS * Y_LOW
HANDS = 2
ROWS = 128
DEPTH = 2048
PER = 32
QUARTERS = CORES * Y_HIGH
QROWS = Z_CHIPS * PER
LANES = 128
PIECES = 8
STACK = 2
PIECE = DEPTH // PIECES
PIECE_ORDER = (0, 4, 1, 5, 2, 6, 3, 7)
CHUNKS = (
    (0, 256, False, "z"),
    (256, 256, False, "z"),
    (512, 256, False, "y"),
    (768, 256, True, "y"),
    (1024, 256, False, "z"),
    (1280, 256, False, "y"),
    (1536, 256, False, "z"),
    (1792, 256, False, "y"),
)
ORDER = (
    (1, 0), (2, 0), (0, 0), (4, 0), (6, 0), (5, 0), (3, 0), (1, 1), (2, 1), (0, 1), (2, 2), (4, 1),
    (7, 0), (6, 1), (1, 2), (5, 1), (0, 2), (3, 1), (4, 2), (2, 3), (6, 2), (7, 1), (1, 3), (0, 3),
    (5, 2), (3, 2), (4, 3), (2, 4), (5, 3), (3, 3), (6, 3), (7, 2), (7, 3), (1, 4), (4, 4), (3, 4),
    (5, 4), (7, 4), (6, 4), (2, 5), (0, 4), (3, 5), (5, 5), (1, 5), (7, 5), (4, 5), (2, 6), (0, 5),
    (6, 5), (3, 6), (5, 6), (7, 6), (4, 6), (2, 7), (0, 6), (6, 6), (1, 6), (5, 7), (3, 7), (7, 7),
)
STAT_SLOT = {1: 1, 2: 3, 3: 2, 4: 4, 5: 5, 6: 7, 7: 6}

f32 = jnp.float32
bf16 = jnp.bfloat16


def width_of(chunk):
    return chunk[1] + (LANES if chunk[2] else 0)


def kernel(images, precision_hbm, projections, mask_hbm, posteriors, references, precision, tile_mask, raw, xbuf, table, half_squares, bias, lifted,
           weights, turned, given, stat_out, stat_in, ready, load_sem, piece_send, piece_recv, stat_send, stat_recv, post_sem,
           core_send, core_recv, ring_send, ring_recv, y_send, y_recv, *chunk_refs):
    img, ori = lax.axis_index("img"), lax.axis_index("ori")
    z, y_hi, core = img // 4, (img // 2) % 2, img % 2
    x, y_lo = ori // 2, ori % 2

    def at_ori(dx, flip):
        row = 1 - y_lo if flip else y_lo
        return ((x + dx) % X_CHIPS) * 2 + row

    where_from = [at_ori(0, False), at_ori(0, True), at_ori(3, False), at_ori(1, False),
                  at_ori(2, False), at_ori(2, True), at_ori(3, True), at_ori(1, True)]
    peers = [(img, w) for w in where_from]
    y_peer, left, right = peers[1], peers[2], peers[3]
    other_core = (z * 4 + y_hi * 2 + 1 - core, ori)
    z_up = (((z + 1) % Z_CHIPS) * 4 + y_hi * 2 + core, ori)
    z_down = (((z + 7) % Z_CHIPS) * 4 + y_hi * 2 + core, ori)
    y_far = (z * 4 + (1 - y_hi) * 2 + core, ori)

    load_images = []
    for i in PIECE_ORDER:
        span = pl.ds(i * PIECE, PIECE)
        load_images.append(pltpu.make_async_copy(images.at[:, span], raw.at[:, span], load_sem.at[i]))
        load_images[-1].start()
    load_small = [pltpu.make_async_copy(precision_hbm, precision, load_sem.at[PIECES]),
                  pltpu.make_async_copy(mask_hbm, tile_mask, load_sem.at[PIECES + 1])]
    load_table = []
    for c in range(CORES):
        for yy in range(Y_HIGH):
            q = c * Y_HIGH + yy
            load_table.append(
                pltpu.make_async_copy(projections.at[:, yy, c], table.at[q], load_sem.at[PIECES + 2 + q]))

    barrier = pltpu.get_barrier_semaphore()
    y = y_hi * Y_LOW + y_lo
    y_sides = []
    for step in (1, 3):
        there = (y + step) % (Y_HIGH * Y_LOW)
        y_sides.append((z * 4 + (there // Y_LOW) * 2 + core, x * 2 + there % Y_LOW))
    friends = y_sides + [left, right, other_core, z_up, z_down]
    for friend in friends:
        pl.semaphore_signal(barrier, inc=1, device_id=friend, device_id_type=MESH)

    def lower(place):
        load_images[place].wait()
        span = pl.ds(PIECE_ORDER[place] * PIECE, PIECE)
        xbuf[0, :, span] = raw[:, span].astype(bf16)

    for place in range(2):
        lower(place)
    pl.semaphore_wait(barrier, len(friends))
    for side in y_sides:
        pl.semaphore_signal(ready, inc=1, device_id=side, device_id_type=MESH)

    sends = []
    arrivals = {}
    counter = [0]

    def send_piece(slot, piece, target, far_slot):
        span = pl.ds(piece * PIECE, PIECE)
        copy = pltpu.make_async_remote_copy(
            src_ref=xbuf.at[slot, :, span], dst_ref=xbuf.at[far_slot, :, span], send_sem=piece_send.at[counter[0]],
            recv_sem=piece_recv.at[far_slot, piece], device_id=target, device_id_type=MESH)
        counter[0] += 1
        copy.start()
        sends.append(copy)
        arrivals[(far_slot, piece)] = copy

    def arrived(slot, piece):
        arrivals[(slot, piece)].wait_recv()

    half = PIECES // 2
    for i in range(half):
        if i > 0:
            lower(2 * i)
            lower(2 * i + 1)
        send_piece(0, i, right, 2)
        send_piece(0, half + i, left, 3)
        send_piece(0, i, y_peer, 1)
        send_piece(0, half + i, y_peer, 1)
    for i in range(half):
        send_piece(0, half + i, right, 2)
        send_piece(0, i, left, 3)

    for copy in load_small + load_table:
        copy.start()
    for copy in load_small + load_table:
        copy.wait()

    def square_tile(q, carry):
        wide = table[q].reshape(QROWS, DEPTH).astype(f32)
        total = jnp.sum(wide * wide, axis=1, keepdims=True)
        half_squares[q] = jnp.broadcast_to(0.5 * total, (QROWS, LANES))
        return carry

    lax.fori_loop(0, QUARTERS, square_tile, 0)

    row_ids = lax.broadcasted_iota(jnp.int32, (GROUP, LANES), 0)
    state = {"high": jnp.zeros((GROUP, LANES), f32), "total": jnp.zeros((GROUP, LANES), f32)}

    def product_tile(q, slots, spans):
        total = None
        for first, last in spans:
            span = pl.ds(first * PIECE, (last - first) * PIECE)
            block = table[q, :, :, span].reshape(QROWS, (last - first) * PIECE)
            rows = xbuf[pl.ds(slots[0], len(slots)), :, span].reshape(len(slots) * ROWS, (last - first) * PIECE)
            part = lax.dot_general(block, rows, (((1,), (1,)), ((), ())), preferred_element_type=f32)
            total = part if total is None else total + part
        return total

    def partial_score(slots, spans):
        cols = pl.ds(slots[0] * LANES, len(slots) * LANES)

        def tile(t, carry):
            for i in range(STACK):
                q = t * STACK + i
                lifted[q, :, cols] = product_tile(q, slots, spans)
            return carry

        lax.fori_loop(0, QUARTERS // STACK, tile, 0)

    def score(slots, spans=((0, PIECES),), started=False):
        wide = len(slots) * LANES
        cols = pl.ds(slots[0] * LANES, wide)
        for k, slot in enumerate(slots):
            for zz in range(Z_CHIPS):
                live = jnp.where(tile_mask[where_from[slot], zz] > 0, 0.0, very_low)
                bias[pl.ds(zz * PER, PER), pl.ds(k * LANES, LANES)] = jnp.full((PER, LANES), live, f32)
        scale = jnp.concatenate([precision[pl.ds(where_from[slot], 1), :] for slot in slots], axis=1)

        def score_tile(t, high):
            for i in range(STACK):
                q = t * STACK + i
                products = product_tile(q, slots, spans)
                if started:
                    products = products + lifted[q, :, cols]
                norm = jnp.concatenate([half_squares[q]] * len(slots), axis=1)
                scores = scale * (products - norm) + bias[:, 0:wide]
                lifted[q, :, cols] = scores
                high = jnp.maximum(high, jnp.max(scores.reshape(QROWS // 8, 8, wide), axis=0))
            return high

        high = lax.fori_loop(0, QUARTERS // STACK, score_tile, jnp.full((8, wide), -3e38, f32))
        high = jnp.max(high, axis=0, keepdims=True)

        def lift_tile(q, total):
            values = jnp.exp(lifted[q, :, cols] - high)
            lifted[q, :, cols] = values
            return total + jnp.sum(values.reshape(QROWS // 8, 8, wide), axis=0)

        total = lax.fori_loop(0, QUARTERS, lift_tile, jnp.zeros((8, wide), f32))
        total = jnp.sum(total, axis=0, keepdims=True)
        for k, slot in enumerate(slots):
            here = row_ids == where_from[slot]
            span = slice(k * LANES, (k + 1) * LANES)
            state["high"] = jnp.where(here, high[:, span], state["high"])
            state["total"] = jnp.where(here, total[:, span], state["total"])

    def turn(slot):
        span = pl.ds(slot * LANES, LANES)

        def tile(zz, carry):
            rows = pl.ds(pl.multiple_of(zz * PER, PER), PER)
            block = jnp.concatenate([lifted[q, rows, span] for q in (0, 2, 1, 3)], axis=0)
            turned[slot, :, pl.ds(pl.multiple_of(zz * LANES, LANES), LANES)] = block.T
            return carry

        lax.fori_loop(0, Z_CHIPS, tile, 0)

    for i in range(half):
        arrived(2, i)
        send_piece(2, i, right, 4)
        arrived(3, half + i)
        send_piece(3, half + i, left, 4)
        if i == 1:
            score((0,))
    for i in range(half):
        arrived(1, i)
        send_piece(1, i, right, 6)
        arrived(1, half + i)
        send_piece(1, half + i, left, 7)
        arrived(2, half + i)
        send_piece(2, half + i, y_peer, 6)
        arrived(3, i)
        send_piece(3, i, y_peer, 7)
        if i == 0:
            turn(0)
    score((1, 2))
    turn(1)
    turn(2)
    for i in range(half):
        arrived(4, i)
        arrived(4, half + i)
    for i in (3, 6, 7):
        send_piece(4, i, y_peer, 5)
    for i in range(2):
        arrived(6, half + i)
        send_piece(6, half + i, right, 5)
        arrived(7, i)
        send_piece(7, i, left, 5)
    score((3, 4))
    arrived(6, half + 2)
    arrived(7, 2)
    send_piece(7, 2, left, 5)
    turn(3)
    turn(4)
    arrived(6, PIECES - 1)
    arrived(7, half - 1)
    for i in range(half):
        arrived(6, i)
        arrived(7, half + i)
    score((6, 7))
    for i in (4, 0, 5, 1, 3, 6):
        arrived(5, i)
    partial_score((5,), ((0, 2), (3, 7)))
    for i in (2, 7):
        arrived(5, i)
    score((5,), ((2, 3), (7, 8)), True)

    my_high, my_total = state["high"], state["total"]
    stat_out[0:GROUP, :] = my_high
    stat_out[GROUP:2 * GROUP, :] = my_total
    stat_copies = []
    for r in range(1, GROUP):
        copy = pltpu.make_async_remote_copy(
            src_ref=stat_out, dst_ref=stat_in.at[STAT_SLOT[r]], send_sem=stat_send.at[r],
            recv_sem=stat_recv.at[STAT_SLOT[r]], device_id=peers[r], device_id_type=MESH)
        copy.start()
        sends.append(copy)
        stat_copies.append(copy)
    for slot in (6, 7, 5):
        turn(slot)
    for copy in stat_copies:
        copy.wait_recv()
    highest = my_high
    for r in range(1, GROUP):
        highest = jnp.maximum(highest, stat_in[r, 0:GROUP, :])
    my_part = jnp.exp(my_high - highest)
    whole = my_total * my_part
    for r in range(1, GROUP):
        whole = whole + stat_in[r, GROUP:2 * GROUP, :] * jnp.exp(stat_in[r, 0:GROUP, :] - highest)
    factor = my_part / whole
    factor_rows = [jnp.sum(jnp.where(row_ids == w, factor, 0.0), axis=0, keepdims=True) for w in where_from]
    factor_row = jnp.concatenate(factor_rows, axis=1)

    def weight_tile(q, carry):
        weights[q] = (lifted[q] * factor_row).astype(bf16)
        return carry

    lax.fori_loop((1 - core) * Y_HIGH, (1 - core) * Y_HIGH + Y_HIGH, weight_tile, 0)

    post_copies = []

    def give_posteriors(slot):
        columns = jnp.broadcast_to(factor_rows[slot], (LANES, LANES)).T
        for t in range(QUARTERS * QROWS // LANES):
            span = pl.ds(t * LANES, LANES)
            given[slot, :, span] = (turned[slot, :, span] * columns).astype(bf16)
        first = pl.multiple_of(where_from[slot] * ROWS, ROWS)
        copy = pltpu.make_async_copy(given.at[slot], posteriors.at[pl.ds(first, ROWS), :], post_sem.at[slot])
        copy.start()
        post_copies.append(copy)

    per_chunk = [chunk_refs[i * 7:(i + 1) * 7] for i in range(len(CHUNKS))]
    ring_copies = {}
    core_copies, y_copies = {}, {}
    mine_y = core * Y_HIGH

    def product(chunk, q):
        start, wide, counted, _ = chunk
        block = weights[q]
        rows = xbuf[:, :, pl.ds(start, wide)].reshape(GROUP * ROWS, wide)
        value = jnp.dot(block, rows, preferred_element_type=f32)
        if counted:
            ones = jnp.ones((GROUP * ROWS, LANES), bf16)
            value = jnp.concatenate([value, jnp.dot(block, ones, preferred_element_type=f32)], axis=1)
        return value

    def stage_core(j):
        to_core = per_chunk[j][0]
        for yy in range(Y_HIGH):
            to_core[yy] = product(CHUNKS[j], (1 - core) * Y_HIGH + yy).astype(bf16)
        copy = pltpu.make_async_remote_copy(
            src_ref=to_core, dst_ref=per_chunk[j][1], send_sem=core_send.at[j], recv_sem=core_recv.at[j],
            device_id=other_core, device_id_type=MESH)
        copy.start()
        sends.append(copy)
        core_copies[j] = copy

    def ring_start(j, step, up, src, dst):
        d = 0 if up else 1
        copy = pltpu.make_async_remote_copy(
            src_ref=src, dst_ref=dst, send_sem=ring_send.at[j, step, d], recv_sem=ring_recv.at[j, step, d],
            device_id=z_up if up else z_down, device_id_type=MESH)
        copy.start()
        sends.append(copy)
        ring_copies[(j, step, d)] = copy

    def ring_first(j):
        out, into = per_chunk[j][3], per_chunk[j][4]
        rows = out.shape[2]
        mid = rows // 2
        values = local_rows(j, 4).astype(bf16)
        out[0, 0, 0:mid] = values[0:mid]
        out[0, 1, 0:mid] = values[mid:rows]
        for d in range(2):
            ring_start(j, 0, d == 0, out.at[0, d, pl.ds(0, mid)], into.at[0, d, pl.ds(0, mid)])

    def ring_next(j, step):
        out, into = per_chunk[j][3], per_chunk[j][4]
        rows = out.shape[2]
        mid = rows // 2
        for d in range(2):
            mine = local_rows(j, 4 - step if d == 0 else 4 + step)
            ring_copies[(j, step - 1, d)].wait_recv()
            if step == 1:
                got = into[0, d, 0:mid].astype(f32)
                if d == 0:
                    out[1, d, 0:mid] = (mine[0:mid] + got).astype(bf16)
                    out[1, d, mid:rows] = mine[mid:rows].astype(bf16)
                else:
                    out[1, d, 0:mid] = mine[0:mid].astype(bf16)
                    out[1, d, mid:rows] = (mine[mid:rows] + got).astype(bf16)
            else:
                out[step, d] = (mine + into[step - 1, d].astype(f32)).astype(bf16)
            ring_start(j, step, d == 0, out.at[step, d], into.at[step, d])

    def ring_sum(j):
        into = per_chunk[j][4]
        mine = local_rows(j, 0)
        for d in range(2):
            ring_copies[(j, 3, d)].wait_recv()
        return mine + into[3, 0].astype(f32) + into[3, 1].astype(f32)

    def y_start(j):
        copy = pltpu.make_async_remote_copy(
            src_ref=per_chunk[j][5], dst_ref=per_chunk[j][6], send_sem=y_send.at[j, 0], recv_sem=y_recv.at[j, 0],
            device_id=y_far, device_id_type=MESH)
        copy.start()
        sends.append(copy)
        y_copies[j] = copy

    def y_slices(j, steps):
        for step in steps:
            which = (z + step) % Z_CHIPS
            copy = pltpu.make_async_remote_copy(
                src_ref=per_chunk[j][5].at[which], dst_ref=per_chunk[j][6].at[which], send_sem=y_send.at[j, step],
                recv_sem=y_recv.at[j, step], device_id=y_far, device_id_type=MESH)
            copy.start()
            sends.append(copy)
            y_copies[(j, step)] = copy

    def local_rows(j, step):
        which = (z + step) % Z_CHIPS
        if CHUNKS[j][3] == "z":
            return per_chunk[j][2][which]
        y_copies[(j, step)].wait_recv()
        return per_chunk[j][2][which] + per_chunk[j][6][which].astype(f32)

    def stage_local(j):
        from_core, local = per_chunk[j][1], per_chunk[j][2]
        wide = width_of(CHUNKS[j])
        z_first = CHUNKS[j][3] == "z"

        def own(yy):
            value = product(CHUNKS[j], mine_y + yy) + from_core[yy].astype(f32)
            return value.reshape(Z_CHIPS, PER, wide)

        core_copies[j].wait_recv()
        if z_first:
            for yy in range(Y_HIGH):
                local[:, pl.ds(yy * PER, PER), :] = own(yy)
            ring_first(j)
        else:
            per_chunk[j][5][...] = own(1 - y_hi).astype(bf16)
            local[...] = own(y_hi)
            y_slices(j, (4, 3, 5))

    state["divide"] = None
    waiting = []

    def finish(j, value):
        start, wide, counted, _ = CHUNKS[j]
        if counted:
            state["divide"] = value[:, wide:wide + LANES] + prior_weight
        prior = table[mine_y + y_hi, z, :, pl.ds(start, wide)].astype(f32)
        references[:, pl.ds(start, wide)] = value[:, 0:wide] + prior_weight * prior
        waiting.append((start, wide))
        if state["divide"] is not None:
            for first, columns in waiting:
                below = jnp.concatenate([state["divide"]] * (columns // LANES), axis=1)
                references[:, pl.ds(first, columns)] = references[:, pl.ds(first, columns)] / below
            waiting.clear()

    def stages(j):
        if CHUNKS[j][3] == "z":
            def to_y():
                local = per_chunk[j][2]
                local[z] = ring_sum(j)
                per_chunk[j][5][...] = local[z, pl.ds(pl.multiple_of((1 - y_hi) * PER, PER), PER), :].astype(bf16)
                y_start(j)

            def last():
                y_copies[j].wait_recv()
                mine = per_chunk[j][2][z, pl.ds(pl.multiple_of(y_hi * PER, PER), PER), :]
                finish(j, mine + per_chunk[j][6][...].astype(f32))

            return [lambda: stage_core(j), lambda: stage_local(j), lambda: ring_next(j, 1), lambda: ring_next(j, 2),
                    lambda: ring_next(j, 3), to_y, last]

        return [lambda: stage_core(j), lambda: stage_local(j), lambda: y_slices(j, (2, 6, 1, 7, 0)), lambda: ring_first(j),
                lambda: ring_next(j, 1), lambda: ring_next(j, 2), lambda: ring_next(j, 3), lambda: finish(j, ring_sum(j))]

    pl.semaphore_wait(ready, 2)
    plans = [stages(j) for j in range(len(CHUNKS))]
    for place, (j, s) in enumerate(ORDER):
        plans[j][s]()
        if place == 0:
            lax.fori_loop(core * Y_HIGH, core * Y_HIGH + Y_HIGH, weight_tile, 0)
        if place % 4 == 3 and place // 4 < GROUP:
            give_posteriors(place // 4)

    for copy in sends:
        copy.wait_send()
    for copy in post_copies:
        copy.wait()


def scratch():
    shapes = [
        pltpu.VMEM((GROUP, ROWS), f32),
        pltpu.SMEM((GROUP, Z_CHIPS), jnp.int32),
        pltpu.VMEM((ROWS, DEPTH), f32),
        pltpu.VMEM((GROUP, ROWS, DEPTH), bf16),
        pltpu.VMEM((QUARTERS, Z_CHIPS, PER, DEPTH), bf16),
        pltpu.VMEM((QUARTERS, QROWS, LANES), f32),
        pltpu.VMEM((QROWS, 2 * LANES), f32),
        pltpu.VMEM((QUARTERS, QROWS, GROUP * ROWS), f32),
        pltpu.VMEM((QUARTERS, QROWS, GROUP * ROWS), bf16),
        pltpu.VMEM((GROUP, ROWS, QUARTERS * QROWS), f32),
        pltpu.VMEM((GROUP, ROWS, QUARTERS * QROWS), bf16),
        pltpu.VMEM((2 * GROUP, LANES), f32),
        pltpu.VMEM((GROUP, 2 * GROUP, LANES), f32),
        pltpu.SemaphoreType.REGULAR,
        pltpu.SemaphoreType.DMA((PIECES + 2 + QUARTERS,)),
        pltpu.SemaphoreType.DMA((7 * PIECES,)),
        pltpu.SemaphoreType.DMA((GROUP, PIECES)),
        pltpu.SemaphoreType.DMA((GROUP,)),
        pltpu.SemaphoreType.DMA((GROUP,)),
        pltpu.SemaphoreType.DMA((GROUP,)),
        pltpu.SemaphoreType.DMA((len(CHUNKS),)),
        pltpu.SemaphoreType.DMA((len(CHUNKS),)),
        pltpu.SemaphoreType.DMA((len(CHUNKS), 4, 2)),
        pltpu.SemaphoreType.DMA((len(CHUNKS), 4, 2)),
        pltpu.SemaphoreType.DMA((len(CHUNKS), Z_CHIPS)),
        pltpu.SemaphoreType.DMA((len(CHUNKS), Z_CHIPS)),
    ]
    for chunk in CHUNKS:
        wide = width_of(chunk)
        z_first = chunk[3] == "z"
        rows = Y_HIGH * PER if z_first else PER
        y_shape = (PER, wide) if z_first else (Z_CHIPS, PER, wide)
        shapes += [
            pltpu.VMEM((Y_HIGH, QROWS, wide), bf16),
            pltpu.VMEM((Y_HIGH, QROWS, wide), bf16),
            pltpu.VMEM((Z_CHIPS, rows, wide), f32),
            pltpu.VMEM((4, 2, rows, wide), bf16),
            pltpu.VMEM((4, 2, rows, wide), bf16),
            pltpu.VMEM(y_shape, bf16),
            pltpu.VMEM(y_shape, bf16),
        ]
    return shapes


def hand_over(posts, refs, posts_out, refs_out, sem):
    rows = GROUP * ROWS // HANDS
    spans = [pl.ds(i * rows, rows) for i in range(HANDS)]
    copies = [pltpu.make_async_copy(posts.at[s], posts_out.at[s], sem.at[i]) for i, s in enumerate(spans)]
    copies.append(pltpu.make_async_copy(refs, refs_out, sem.at[HANDS]))
    for copy in copies:
        copy.start()
    for copy in copies:
        copy.wait()


def body(images, precision, projections, tile_mask):
    posts, refs = pl.pallas_call(
        kernel,
        out_shape=(
            jax.ShapeDtypeStruct((GROUP * ROWS, QUARTERS * QROWS), bf16),
            jax.ShapeDtypeStruct((PER, DEPTH), f32),
        ),
        in_specs=[
            pl.BlockSpec(memory_space=pltpu.HBM),
            pl.BlockSpec(memory_space=pltpu.HBM),
            pl.BlockSpec(memory_space=pltpu.HBM),
            pl.BlockSpec(memory_space=pltpu.HBM),
        ],
        out_specs=(pl.BlockSpec(memory_space=pl.ANY), pl.BlockSpec(memory_space=pltpu.VMEM)),
        scratch_shapes=scratch(),
        compiler_params=pltpu.CompilerParams(
            collective_id=0, has_side_effects=True, vmem_limit_bytes=40 * 1024 * 1024
        ),
    )(*[pltpu.with_memory_space_constraint(v, pltpu.HBM) for v in (images, precision.reshape(GROUP, ROWS), projections.reshape(Z_CHIPS, Y_HIGH, CORES, PER, DEPTH), tile_mask)])
    return pl.pallas_call(
        hand_over,
        out_shape=(jax.ShapeDtypeStruct(posts.shape, bf16), jax.ShapeDtypeStruct(refs.shape, f32)),
        in_specs=[pl.BlockSpec(memory_space=pl.ANY)] * 2,
        out_specs=(pl.BlockSpec(memory_space=pltpu.HBM), pl.BlockSpec(memory_space=pltpu.HBM)),
        scratch_shapes=[pltpu.SemaphoreType.DMA((HANDS + 1,))],
        compiler_params=pltpu.CompilerParams(vmem_limit_bytes=4 * 1024 * 1024),
    )(posts, refs)


def solution(mesh):
    return jax.shard_map(
        body,
        mesh=mesh,
        in_specs=(P(("img", "ori"), None), P("img"), P("ori", None), P("img", "ori")),
        out_specs=(P("img", "ori"), P(("ori", "img"), None)),
        check_vma=False,
    )
```
